256 devices in a mesh: blk: 16 (over z, x_lo), mode: 16 (over y, x_hi, core).
Axes of the slice: x: 4 (x_hi: 2, x_lo: 2; x = x_hi * 2 + x_lo), y: 4, z: 8, core: 2. Of those that a mesh axis runs over, the one named last changes fastest.
Arguments:
- chaos_field: float32 [448, 65536], P('mode', 'blk'), may hold values from -6 to 6
- kl_field: float32 [13, 65536], P(None, 'blk'), may hold values from -1.6 to 4, as said below
- partner: int32 [12, 2, 448], P(None, None, 'mode'), may hold values from 0 to 447, each once within a row
- chaos_coef: float32 [12, 2, 448], P(None, None, 'mode'), may hold values from 0.5 to 2
- cell_count: int32 [16], P('blk'), may hold values from 2048 to 4096, as said below
- face_count: int32 [16, 4], P('blk'), may hold values from 0 to 128, as said below
- face_cells: int32 [16, 4, 128], P('blk'), may hold values from 0 to 4095, as said below
Outputs:
- applied: float32 [448, 65536], P('mode', 'blk')
The draws below stay inside these ranges and needn't reach their ends.
Inputs may be any that keep to these rules, and one draw needn't show every extreme that they name: A block's live cells are its first cell_count cells, a whole number of rows of 128; some block is full. `face_count`: slots are the neighbouring blocks at offsets -2, -1, +1, +2 of the block index; a pair of blocks has the same count seen from either side, and 0 where the neighbour does not exist. `face_cells`: entry f of a slot pairs with entry f of the neighbour's opposite slot; entries below the count name live cells. `kl_field`: row 0 lies in 0.5 to 4.
All inputs are finite; a program needn't handle non-finite values.
Results may differ from the reference program's by a relative error of at most 0.000068.
Values sent between devices are 32-bit elements; how exact they have to be, the bound alone decides.
No kernel may reach another device: no remote copies, remote signals or barrier semaphores. Data moves between devices by JAX's collectives and lax.ppermute only.
A program may use at most 64 MiB of HBM per device.

```python
import math
import jax
import jax.numpy as jnp
from jax import lax

GX = 32
GZ = 128
MODES = 448
KL = 12
FACE_MAX = 128
NBLK = 16
CELLS = 65536


def block_layout(key):
    folded = jax.random.fold_in(key, 41)
    key_rows, key_full, key_count, key_pick, key_low, key_high = jax.random.split(folded, 6)
    block_ids = jnp.arange(NBLK, dtype=jnp.int32)
    grid_rows = jax.random.randint(key_rows, (NBLK,), GX // 2, GX + 1)
    full_block = jax.random.randint(key_full, (), 0, NBLK)
    grid_rows = jnp.where(block_ids == full_block, GX, grid_rows)
    alive_cells = (grid_rows * GZ).astype(jnp.int32)
    pair_count = jax.random.randint(key_count, (NBLK, 2), 0, FACE_MAX + 1)
    widest = jax.random.randint(key_pick, (), 0, NBLK - 1)
    pair_count = jnp.where((block_ids[:, None] == widest) & (jnp.arange(2)[None, :] == 0), FACE_MAX, pair_count)
    partner_ids = block_ids[:, None] + jnp.arange(1, 3, dtype=jnp.int32)[None, :]
    pair_count = jnp.where(partner_ids < NBLK, pair_count, 0).astype(jnp.int32)
    low_cells = jax.random.randint(key_low, (NBLK, 2, FACE_MAX), 0, 1 << 30) % alive_cells[:, None, None]
    partner_alive = alive_cells[jnp.minimum(partner_ids, NBLK - 1)]
    high_cells = jax.random.randint(key_high, (NBLK, 2, FACE_MAX), 0, 1 << 30) % partner_alive[:, :, None]
    return (alive_cells, pair_count, low_cells.astype(jnp.int32), high_cells.astype(jnp.int32))


def shift_down(values, distance):
    return jnp.concatenate([jnp.zeros_like(values[:distance]), values[:-distance]], axis=0)[:values.shape[0]]


def draw_cell_count(key, part):
    return block_layout(key)[0]


def draw_face_count(key, part):
    pair_count = block_layout(key)[1]
    return jnp.stack([shift_down(pair_count[:, 1], 2), shift_down(pair_count[:, 0], 1), pair_count[:, 0], pair_count[:, 1]], axis=1).astype(jnp.int32)


def draw_face_cells(key, part):
    layout = block_layout(key)
    low_cells = layout[2]
    high_cells = layout[3]
    return jnp.stack([shift_down(high_cells[:, 1], 2), shift_down(high_cells[:, 0], 1), low_cells[:, 0], low_cells[:, 1]], axis=1).astype(jnp.int32)


def draw_kl_field(key, part):
    key_mean, key_terms = jax.random.split(jax.random.fold_in(key, 5))
    mean_row = jnp.exp(jax.random.uniform(key_mean, (1, CELLS), jnp.float32, math.log(0.5), math.log(4.0)))
    term_rows = jnp.clip(0.4 * jax.random.normal(key_terms, (KL, CELLS), jnp.float32), -1.6, 1.6)
    return jnp.concatenate([mean_row, term_rows], axis=0).astype(jnp.float32)


def levels(key, shape, shards, smallest, high):
    loudness, own = 1.0, jax.random.fold_in(key, 6)
    for axis_at, blocks in shards:
        steps = jnp.exp(jax.random.uniform(jax.random.fold_in(own, axis_at), (blocks,), jnp.float32, smallest / len(shards), high / len(shards)))
        loudness = loudness * jnp.repeat(steps, shape[axis_at] // blocks).reshape([-1 if axis == axis_at else 1 for axis in range(len(shape))])
    return loudness


def scatter_about(stream_key, extent, spread, bound, shards=(), held_as=jnp.bfloat16):
    factor_of = levels(stream_key, extent, shards, -0.22, 0.18) if shards else 1.0
    drawn = jax.random.normal(stream_key, extent, jnp.float32) * spread * factor_of
    return jnp.minimum(jnp.maximum(drawn, -bound), bound).astype(held_as)


def setup_inputs(seed: int = 0) -> dict:
    arg_keys = jax.random.split(jax.random.key(seed), 8)
    chaos_field = scatter_about(arg_keys[0], (MODES, CELLS), 1.0, 6.0, ((0, 16), (1, 16)), jnp.float32)
    kl_field = draw_kl_field(jax.random.fold_in(arg_keys[7], 71), 0)
    partner = jax.vmap(lambda own: jax.random.permutation(own, MODES))(jax.random.split(arg_keys[2], KL * 2)).reshape((KL, 2, MODES)).astype(jnp.int32)
    chaos_coef = jnp.clip(0.5 + 1.5 * jax.random.uniform(arg_keys[3], (KL, 2, MODES), jnp.float32) ** levels(arg_keys[3], (KL, 2, MODES), ((2, 16),), -0.2, 0.2), 0.5, 2.0)
    cell_count = draw_cell_count(jax.random.fold_in(arg_keys[7], 71), 0)
    face_count = draw_face_count(jax.random.fold_in(arg_keys[7], 71), 0)
    face_cells = draw_face_cells(jax.random.fold_in(arg_keys[7], 71), 0)
    return dict(chaos_field=chaos_field, kl_field=kl_field, partner=partner, chaos_coef=chaos_coef, cell_count=cell_count, face_count=face_count, face_cells=face_cells)


SLOT_OFFSETS = (-2, -1, 1, 2)


def grid_terms(values, conduct, alive_grid):
    down_coef = 0.5 * (conduct[..., 1:, :] + conduct[..., :-1, :]) * (alive_grid[..., 1:, :] * alive_grid[..., :-1, :])
    down_step = down_coef * (values[..., :-1, :] - values[..., 1:, :])
    side_coef = 0.5 * (conduct[..., :, 1:] + conduct[..., :, :-1]) * (alive_grid[..., :, 1:] * alive_grid[..., :, :-1])
    side_step = side_coef * (values[..., :, :-1] - values[..., :, 1:])
    leading = [(0, 0)] * (values.ndim - 2)
    result = jnp.pad(down_step, leading + [(0, 1), (0, 0)]) - jnp.pad(down_step, leading + [(1, 0), (0, 0)])
    return result + jnp.pad(side_step, leading + [(0, 0), (0, 1)]) - jnp.pad(side_step, leading + [(0, 0), (1, 0)])


def reference(chaos_field, kl_field, partner, chaos_coef, cell_count, face_count, face_cells):
    cells_block = GX * GZ
    alive_flag = (lax.iota(jnp.int32, cells_block)[None, :] < cell_count[:, None]).astype(jnp.float32)
    alive_grid = alive_flag.reshape(NBLK, GX, GZ)
    alive_flat = alive_flag.reshape(1, -1)
    masked = chaos_field * alive_flat
    block_ids = jnp.arange(NBLK, dtype=jnp.int32)
    own_index = (block_ids[:, None, None] * cells_block + face_cells).reshape(-1).astype(jnp.int32)
    remote_list = []
    for slot_index, offset in enumerate(SLOT_OFFSETS):
        neighbour = jnp.clip(block_ids + offset, 0, NBLK - 1).astype(jnp.int32)
        remote_list.append(neighbour[:, None] * cells_block + face_cells[neighbour, 3 - slot_index])
    remote_index = jnp.stack(remote_list, axis=1).reshape(-1).astype(jnp.int32)
    face_alive = (lax.iota(jnp.int32, FACE_MAX)[None, None, :] < face_count[:, :, None]).astype(jnp.float32).reshape(-1)
    summed = jnp.zeros((MODES, CELLS), jnp.float32)
    for kl_index in range(KL + 1):
        if kl_index == 0:
            mixed_field = masked
        else:
            pairs = partner[kl_index - 1]
            weights = chaos_coef[kl_index - 1]
            mixed_field = weights[0][:, None] * masked[pairs[0]] + weights[1][:, None] * masked[pairs[1]]
        conduct = kl_field[kl_index]
        grid_part = grid_terms(mixed_field.reshape(MODES, NBLK, GX, GZ), conduct.reshape(NBLK, GX, GZ), alive_grid)
        face_coef = 0.5 * (conduct[own_index] + conduct[remote_index]) * face_alive
        face_part = face_coef[None, :] * (mixed_field[:, own_index] - mixed_field[:, remote_index])
        summed = summed + grid_part.reshape(MODES, CELLS)
        summed = summed.at[:, own_index].add(face_part)
    return summed * alive_flat
```

```python
import jax
import jax.numpy as jnp
from jax import lax
from jax.experimental import pallas as pl
from jax.experimental.pallas import tpu as pltpu
from jax.sharding import PartitionSpec as P

SLOT_OFFSETS = (-2, -1, 1, 2)
F32 = jnp.float32
BF16 = jnp.bfloat16


def lanes(value, shift):
    shift = shift % 128
    return value if shift == 0 else pltpu.roll(value, shift, 1)


def lane_ids(rows):
    return lax.broadcasted_iota(jnp.int32, (rows, 128), 1)


def along(value, index):
    return jnp.take_along_axis(value, index, axis=1, mode="promise_in_bounds")


def pack_tiles(source_ref, rows, face_row, face_lane, out_ref):
    lane = lane_ids(rows)
    group = lane >> 5
    for mr in range(4):
        for v in range(2):
            cells = [source_ref[:, pl.ds(128 * (8 * mr + 4 * v + j), 128)] for j in range(4)]
            for ml in range(4):
                tile = lanes(cells[0], -32 * ml)
                for j in range(1, 4):
                    tile = jnp.where(group == j, lanes(cells[j], 32 * (j - ml)), tile)
                out_ref[4 * mr + ml, :, pl.ds(128 * v, 128)] = tile
    faces = [jnp.zeros((rows, 128), F32) for _ in range(4)]
    picks = [jnp.broadcast_to(face_lane[s : s + 1], (rows, 128)) for s in range(4)]
    for r in range(32):
        cells = source_ref[:, pl.ds(128 * r, 128)]
        for s in range(4):
            faces[s] = jnp.where(face_row[s : s + 1] == r, along(cells, picks[s]), faces[s])
    left_pick = jnp.where((lane >= 64) & (lane < 72), 32 * (lane & 3) + 31, 0)
    right_pick = jnp.where((lane >= 72) & (lane < 80), 32 * (lane & 3), 0)
    for mr in range(4):
        for ml in range(4):
            m = 4 * mr + ml
            halo = jnp.where(lane >= 96, lanes(faces[mr], 96 - 32 * ml), 0.0)
            if mr > 0:
                halo = jnp.where(lane < 32, lanes(out_ref[m - 4, :, pl.ds(128, 128)], 32), halo)
            if mr < 3:
                below = lanes(out_ref[m + 4, :, pl.ds(0, 128)], 32)
                halo = jnp.where((lane >= 32) & (lane < 64), below, halo)
            for v in range(2):
                if ml > 0:
                    side = along(out_ref[m - 1, :, pl.ds(128 * v, 128)], left_pick)
                    halo = jnp.where((lane >= 64 + 4 * v) & (lane < 68 + 4 * v), side, halo)
                if ml < 3:
                    side = along(out_ref[m + 1, :, pl.ds(128 * v, 128)], right_pick)
                    halo = jnp.where((lane >= 72 + 4 * v) & (lane < 76 + 4 * v), side, halo)
            out_ref[m, :, pl.ds(256, 128)] = halo


def pack_kernel(
    count_ref, field_ref, kl_ref, cells_ref, partner_ref, coef_ref, send_ref, klp_ref, field_pad, kl_pad, table
):
    count = count_ref[0]
    lane = lane_ids(28)
    for r in range(32):
        at = pl.ds(128 * r, 128)
        field_pad[0:28, at] = jnp.where(lane + 128 * r < count, field_ref[:, at], 0.0)
    field_pad[28:32, :] = jnp.zeros((4, 4096), F32)
    kl_pad[0:13, :] = kl_ref[...]
    kl_pad[13:16, :] = jnp.zeros((3, 4096), F32)
    face_row = cells_ref[...] >> 7
    face_lane = cells_ref[...] & 127
    pack_tiles(field_pad, 32, face_row, face_lane, send_ref)
    pack_tiles(kl_pad, 16, face_row, face_lane, klp_ref)
    table[0:2, :] = jnp.full((2, 384), -1.0, F32)
    table[2:4, :] = jnp.zeros((2, 384), F32)
    for k in range(12):
        mode = partner_ref[k]
        table[0:2, 32 * k : 32 * k + 28] = (mode + 4 * ((mode * 2341) >> 16)).astype(F32)
        table[2:4, 32 * k : 32 * k + 28] = coef_ref[k]
    for m in range(16):
        send_ref[m, 28:32, :] = table[...]


def face_kernel(halo_ref, klp_ref, out_ref):
    me = lax.axis_index("mode")
    group = lane_ids(8) >> 5
    for t in range(16):
        packed = halo_ref[12 + t // 4, 8 * (t % 4) : 8 * (t % 4) + 8, :]
        for g in range(3):
            piece = halo_ref[4 * g + t // 4, 8 * (t % 4) : 8 * (t % 4) + 8, :]
            packed = jnp.where(group == g, lanes(piece, 32 * g - 96), packed)
        out_ref[8 * t : 8 * t + 8, :] = packed
    out_ref[128:144, :] = klp_ref[me, :, 256:384]


def neighbours(first, second, halo):
    rows = first.shape[0]
    lane = lane_ids(rows)
    up_first, up_second = lanes(first, 32), lanes(second, 32)
    down_first, down_second = lanes(first, -32), lanes(second, -32)
    up = (jnp.where(lane < 32, halo, up_first), jnp.where(lane < 32, up_first, up_second))
    down = (jnp.where(lane < 96, down_first, down_second), jnp.where(lane < 96, down_second, lanes(halo, 64)))
    column = lane & 31
    left, right = [], []
    for v, cells in enumerate((first, second)):
        left_halo = along(halo, 64 + 4 * v + (lane >> 5))
        right_halo = along(halo, 72 + 4 * v + (lane >> 5))
        left.append(jnp.where(column == 0, left_halo, lanes(cells, 1)))
        right.append(jnp.where(column == 31, right_halo, lanes(cells, -1)))
    return up, down, left, right


def apply_kernel(
    count_ref, faces_ref, field_ref, remote_ref, klp_ref, out_ref,
    steps, face_steps, coefs, face_coefs, pays, columns, mix_hi, mix_lo, w_hi, w_lo, w_face, total, face_total,
):
    me = lax.axis_index("mode")
    mr, ml = me // 4, me % 4
    count = count_ref[0]
    lane = lane_ids(16)
    a = [klp_ref[me, :, pl.ds(128 * v, 128)] for v in range(3)]
    around = neighbours(*a)
    for v in range(2):
        row = 8 * mr + 4 * v + (lane >> 5)
        column = 32 * ml + (lane & 31)
        cell = 128 * row + column
        here = cell < count
        there = (
            (row > 0) & (cell - 128 < count),
            (row < 31) & (cell + 128 < count),
            (column > 0) & (cell - 1 < count),
            (column < 127) & (cell + 1 < count),
        )
        for d in range(4):
            value = 0.5 * (a[v] + around[d][v])
            coefs[d, :, pl.ds(128 * v, 128)] = jnp.where(here & there[d], value, 0.0)
    face = 32 * ml + lane - 96
    live = (lane >= 96) & (face < faces_ref[mr])
    face_coefs[...] = jnp.where(live, 0.5 * (a[2] + remote_ref[128:144, :]), 0.0)
    wide = lane_ids(32)
    for s in range(16):
        rows = pl.ds(32 * s, 32)
        cells = [field_ref[s, :, pl.ds(128 * v, 128)] for v in range(3)]
        around = neighbours(*cells)
        for d in range(4):
            for v in range(2):
                steps[d, rows, pl.ds(128 * v, 128)] = cells[v] - around[d][v]
        g = s // 4
        remote = lanes(remote_ref[pl.ds(32 * (s % 4), 32), :], 96 - 32 * g)
        face_steps[rows, :] = jnp.where(wide >= 96, cells[2] - remote, 0.0)
    for t in range(4):
        pays[16 * t : 16 * t + 16, :] = field_ref[:, 28 + t, :]
    same = pays[0:16, :] == pays[16:32, :]
    pays[32:48, :] = pays[32:48, :] + jnp.where(same, pays[48:64, :], 0.0)
    for c in range(3):
        block = jnp.concatenate([pays[:, 128 * c : 128 * c + 128], jnp.zeros((64, 128), F32)], axis=0)
        columns[128 * c : 128 * c + 128, :] = block.T

    def stencil(k, rows):
        w = coefs[0, pl.ds(k, 1), :] * steps[0, rows, :]
        for d in range(1, 4):
            w = w + coefs[d, pl.ds(k, 1), :] * steps[d, rows, :]
        return w

    for s in range(16):
        rows = pl.ds(32 * s, 32)
        total[rows, :] = stencil(0, rows)
        face_total[rows, :] = face_coefs[0:1, :] * face_steps[rows, :]
    target = lax.broadcasted_iota(jnp.int32, (32, 512), 1).astype(F32)

    def term(k, carry):
        at = pl.ds(pl.multiple_of(32 * (k - 1), 32), 32)
        for s in range(16):
            rows = pl.ds(32 * s, 32)
            first, second = (columns[at, 16 * t + s : 16 * t + s + 1] == target for t in range(2))
            coef = [columns[at, 16 * t + s : 16 * t + s + 1] for t in (2, 3)]
            high = [c.astype(BF16).astype(F32) for c in coef]
            low = [c - h for c, h in zip(coef, high)]
            mix_hi[rows, :] = jnp.where(first, high[0], jnp.where(second, high[1], 0.0)).astype(BF16)
            mix_lo[rows, :] = jnp.where(first, low[0], jnp.where(second, low[1], 0.0)).astype(BF16)
            w = stencil(k, rows)
            high = w.astype(BF16)
            w_hi[rows, :] = high
            w_lo[rows, :] = (w - high.astype(F32)).astype(BF16)
            w = face_coefs[pl.ds(k, 1), :] * face_steps[rows, :]
            high = w.astype(BF16).astype(F32)
            w_face[rows, :] = (high + lanes(w - high, -32)).astype(BF16)
        dot = lambda x, y: jnp.dot(x[...], y[...], preferred_element_type=F32)
        total[...] += dot(mix_hi, w_hi) + dot(mix_hi, w_lo) + dot(mix_lo, w_hi)
        face_total[...] += dot(mix_hi, w_face) + dot(mix_lo, w_face)
        return carry

    lax.fori_loop(1, 13, term, 0)
    sub = lax.broadcasted_iota(jnp.int32, (8, 128), 0)
    group = lane_ids(8) >> 5
    for s in range(16):
        for v in range(2):
            at = pl.ds(128 * v, 128)
            out_ref[s, 0:24, at] = total[32 * s : 32 * s + 24, at]
            packed = total[32 * s + 24 : 32 * s + 32, at]
            for u in range(4 * v, min(4 * v + 4, 7)):
                flux = face_total[32 * s + 8 * (u // 2) : 32 * s + 8 * (u // 2) + 8, :]
                flux = flux + lanes(flux, 32)
                if u % 2 == 0:
                    flux = pltpu.roll(flux, 4, 0)
                packed = jnp.where((sub >= 4) & (group == u % 4), lanes(flux, 32 * (u % 4) - 96), packed)
            out_ref[s, 24:32, at] = packed


def unpack_kernel(count_ref, tiles_ref, cells_ref, out_ref, flux, left_hi, left_lo, added):
    count = count_ref[0]
    sub = lax.broadcasted_iota(jnp.int32, (8, 128), 0)
    group = lane_ids(8) >> 5
    for s in range(4):
        for tau in range(4):
            value = jnp.zeros((8, 128), F32)
            for q in range(4):
                m = 4 * s + q
                low = tiles_ref[m, 24:32, pl.ds(128 * (tau // 2), 128)]
                even = pltpu.roll(lanes(low, 32 * (q - (2 * tau) % 4)), 4, 0)
                odd = lanes(low, 32 * (q - (2 * tau + 1) % 4))
                value = jnp.where(group == q, jnp.where(sub < 4, even, odd), value)
            if tau == 3:
                value = jnp.where(sub < 4, value, 0.0)
            flux[8 * tau : 8 * tau + 8, pl.ds(128 * s, 128)] = value
    face_row = [cells_ref[s : s + 1, :] >> 7 for s in range(4)]
    high = [flux[:, pl.ds(128 * s, 128)].astype(BF16).astype(F32) for s in range(4)]
    low = [flux[:, pl.ds(128 * s, 128)] - high[s] for s in range(4)]
    for r in range(32):
        for s in range(4):
            at = (pl.ds(32 * r, 32), pl.ds(128 * s, 128))
            left_hi[at] = jnp.where(face_row[s] == r, high[s], 0.0).astype(BF16)
            left_lo[at] = jnp.where(face_row[s] == r, low[s], 0.0).astype(BF16)
    column = lax.broadcasted_iota(jnp.int32, (128, 128), 0)
    pick = jnp.concatenate(
        [jnp.where((cells_ref[s : s + 1, :] & 127) == column, 1.0, 0.0) for s in range(4)], axis=1
    ).astype(BF16)
    spread = lambda x: lax.dot_general(x[...], pick, (((1,), (1,)), ((), ())), preferred_element_type=F32)
    added[...] = spread(left_hi) + spread(left_lo)
    lane = lane_ids(32)
    group = lane >> 5
    for mr in range(4):
        for v in range(2):
            tiles = [tiles_ref[4 * mr + ml, :, pl.ds(128 * v, 128)] for ml in range(4)]
            for j in range(4):
                row = 8 * mr + 4 * v + j
                value = lanes(tiles[0], -32 * j)
                for ml in range(1, 4):
                    value = jnp.where(group == ml, lanes(tiles[ml], 32 * (ml - j)), value)
                value = value + added[32 * row : 32 * row + 32, :]
                value = jnp.where(lane + 128 * row < count, value, 0.0)
                out_ref[:, pl.ds(128 * row, 128)] = value[0:28]


def face_route(blocks):
    route = []
    for b in range(blocks):
        for s, offset in enumerate(SLOT_OFFSETS):
            if 0 <= b + offset < blocks:
                for q in range(4):
                    route.append((16 * b + 4 * s + q, 16 * (b + offset) + 4 * (3 - s) + q))
    return route


def per_device(chaos_field, kl_field, partner, chaos_coef, cell_count, face_count, face_cells):
    vmem = pl.BlockSpec(memory_space=pltpu.VMEM)
    smem = pl.BlockSpec(memory_space=pltpu.SMEM)
    params = pltpu.CompilerParams(vmem_limit_bytes=56 << 20)
    cells = face_cells[0]
    send, klp = pl.pallas_call(
        pack_kernel,
        out_shape=(jax.ShapeDtypeStruct((16, 32, 384), F32), jax.ShapeDtypeStruct((16, 16, 384), F32)),
        in_specs=[smem] + [vmem] * 5,
        out_specs=(vmem, vmem),
        scratch_shapes=[pltpu.VMEM((32, 4096), F32), pltpu.VMEM((16, 4096), F32), pltpu.VMEM((4, 384), F32)],
        compiler_params=params,
        name="pack",
    )(cell_count, chaos_field, kl_field, cells, partner, chaos_coef)
    field = lax.all_to_all(send, "mode", 0, 0, tiled=True)
    outgoing = pl.pallas_call(
        face_kernel,
        out_shape=jax.ShapeDtypeStruct((144, 128), F32),
        grid=(1,),
        in_specs=[
            pl.BlockSpec((16, 32, 128), lambda i: (0, 0, 2)),
            pl.BlockSpec((16, 16, 384), lambda i: (0, 0, 0)),
        ],
        out_specs=pl.BlockSpec((144, 128), lambda i: (0, 0)),
        compiler_params=params,
        name="faces",
    )(field, klp)
    remote = lax.ppermute(outgoing, ("blk", "mode"), face_route(lax.axis_size("blk")))
    tiles = pl.pallas_call(
        apply_kernel,
        out_shape=jax.ShapeDtypeStruct((16, 32, 256), F32),
        in_specs=[smem, smem, vmem, vmem, vmem],
        out_specs=vmem,
        scratch_shapes=[
            pltpu.VMEM((4, 512, 256), F32),
            pltpu.VMEM((512, 128), F32),
            pltpu.VMEM((4, 16, 256), F32),
            pltpu.VMEM((16, 128), F32),
            pltpu.VMEM((64, 384), F32),
            pltpu.VMEM((384, 128), F32),
            pltpu.VMEM((512, 512), BF16),
            pltpu.VMEM((512, 512), BF16),
            pltpu.VMEM((512, 256), BF16),
            pltpu.VMEM((512, 256), BF16),
            pltpu.VMEM((512, 128), BF16),
            pltpu.VMEM((512, 256), F32),
            pltpu.VMEM((512, 128), F32),
        ],
        compiler_params=params,
        name="apply",
    )(cell_count, face_count[0], field, remote, klp)
    back = lax.all_to_all(tiles, "mode", 0, 0, tiled=True)
    return pl.pallas_call(
        unpack_kernel,
        out_shape=jax.ShapeDtypeStruct(chaos_field.shape, F32),
        in_specs=[smem, vmem, vmem],
        out_specs=vmem,
        scratch_shapes=[
            pltpu.VMEM((32, 512), F32),
            pltpu.VMEM((1024, 512), BF16),
            pltpu.VMEM((1024, 512), BF16),
            pltpu.VMEM((1024, 128), F32),
        ],
        compiler_params=params,
        name="unpack",
    )(cell_count, back, cells)


def solution(mesh):
    in_specs = (
        P("mode", "blk"),
        P(None, "blk"),
        P(None, None, "mode"),
        P(None, None, "mode"),
        P("blk"),
        P("blk", None),
        P("blk", None, None),
    )
    return jax.shard_map(
        per_device, mesh=mesh, in_specs=in_specs, out_specs=P("mode", "blk"), check_vma=False
    )
```

```python
import jax
import jax.numpy as jnp
from jax import lax
from jax.experimental import pallas as pl
from jax.experimental.pallas import tpu as pltpu
from jax.sharding import PartitionSpec as P

SLOT_OFFSETS = (-2, -1, 1, 2)
F32 = jnp.float32
BF16 = jnp.bfloat16
TERMS = 12
MODES = 448
PARTS = 16
HERE = MODES // PARTS
DEPTH = TERMS * MODES
CHUNK = 768


def lanes(value, shift):
    shift = shift % 128
    return value if shift == 0 else pltpu.roll(value, shift, 1)


def lane_ids(rows):
    return lax.broadcasted_iota(jnp.int32, (rows, 128), 1)


def along(value, index):
    return jnp.take_along_axis(value, index, axis=1, mode="promise_in_bounds")


def group_of(v):
    return pl.ds(128 * v, 128)


def pick_faces(source, rows, face_row, face_lane):
    faces = [jnp.zeros((rows, 128), F32) for _ in range(4)]
    picks = [jnp.broadcast_to(face_lane[s : s + 1], (rows, 128)) for s in range(4)]
    for r in range(32):
        cells = source[:, group_of(r)]
        for s in range(4):
            faces[s] = jnp.where(face_row[s : s + 1] == r, along(cells, picks[s]), faces[s])
    return faces


def pack_tiles(source_ref, rows, out_ref, table):
    lane = lane_ids(rows)
    group = lane >> 5
    for mr in range(4):
        for v in range(2):
            cells = [source_ref[:, group_of(8 * mr + 4 * v + j)] for j in range(4)]
            for ml in range(4):
                tile = lanes(cells[0], -32 * ml)
                for j in range(1, 4):
                    tile = jnp.where(group == j, lanes(cells[j], 32 * (j - ml)), tile)
                out_ref[4 * mr + ml, 0:rows, group_of(v)] = tile
    left_pick = jnp.where((lane >= 64) & (lane < 72), 32 * (lane & 3) + 31, 0)
    right_pick = jnp.where((lane >= 72) & (lane < 80), 32 * (lane & 3), 0)
    for mr in range(4):
        for ml in range(4):
            m = 4 * mr + ml
            halo = table
            if mr > 0:
                halo = jnp.where(lane < 32, lanes(out_ref[m - 4, 0:rows, group_of(1)], 32), halo)
            if mr < 3:
                below = lanes(out_ref[m + 4, 0:rows, group_of(0)], 32)
                halo = jnp.where((lane >= 32) & (lane < 64), below, halo)
            for v in range(2):
                if ml > 0:
                    side = along(out_ref[m - 1, 0:rows, group_of(v)], left_pick)
                    halo = jnp.where((lane >= 64 + 4 * v) & (lane < 68 + 4 * v), side, halo)
                if ml < 3:
                    side = along(out_ref[m + 1, 0:rows, group_of(v)], right_pick)
                    halo = jnp.where((lane >= 72 + 4 * v) & (lane < 76 + 4 * v), side, halo)
            out_ref[m, 0:rows, group_of(2)] = halo


def pack_kernel(
    count_ref, far_field, cells_ref, far_partner, far_coef, send_ref, field_ref, partner_ref, coef_ref, stage, arrived
):
    copies = [
        pltpu.make_async_copy(far, near, arrived.at[i])
        for i, (far, near) in enumerate(
            ((far_field, field_ref), (far_partner, partner_ref), (far_coef, coef_ref))
        )
    ]
    for copy in copies:
        copy.start()
    stage[...] = jnp.zeros((128, 128), F32)
    copies[1].wait()
    copies[2].wait()
    for k in range(TERMS):
        mode, coef = partner_ref[k], coef_ref[k]
        same = mode[0:1] == mode[1:2]
        stage[80 + k : 81 + k, 0:HERE] = mode[0:1].astype(F32)
        stage[92 + k : 93 + k, 0:HERE] = mode[1:2].astype(F32)
        stage[104 + k : 105 + k, 0:HERE] = coef[0:1] + jnp.where(same, coef[1:2], 0.0)
        stage[116 + k : 117 + k, 0:HERE] = coef[1:2]
    table = stage[...].T[0:HERE]
    copies[0].wait()
    lane = lane_ids(HERE)
    for r in range(32):
        field_ref[:, group_of(r)] = jnp.where(lane + 128 * r < count_ref[0], field_ref[:, group_of(r)], 0.0)
    pack_tiles(field_ref, HERE, send_ref, table)
    cells = cells_ref[...]
    faces = pick_faces(field_ref, HERE, cells >> 7, cells & 127)
    group = lane_ids(4) >> 5
    for s in range(4):
        turned = [lanes(faces[s], 32 * t) for t in range(4)]
        for q in range(4):
            for v in range(2):
                packed = jnp.zeros((4, 128), F32)
                for u in range(4 * v, min(4 * v + 4, 7)):
                    packed = jnp.where(group == u % 4, turned[(u - q) % 4][4 * u : 4 * u + 4], packed)
                send_ref[4 * s + q, HERE:32, group_of(v)] = packed
            send_ref[4 * s + q, HERE:32, group_of(2)] = jnp.zeros((4, 128), F32)


def neighbours(first, second, halo):
    rows = first.shape[0]
    lane = lane_ids(rows)
    up_first, up_second = lanes(first, 32), lanes(second, 32)
    down_first, down_second = lanes(first, -32), lanes(second, -32)
    up = (jnp.where(lane < 32, halo, up_first), jnp.where(lane < 32, up_first, up_second))
    down = (jnp.where(lane < 96, down_first, down_second), jnp.where(lane < 96, down_second, lanes(halo, 64)))
    column = lane & 31
    left, right = [], []
    for v, cells in enumerate((first, second)):
        left_halo = along(halo, 64 + 4 * v + (lane >> 5))
        right_halo = along(halo, 72 + 4 * v + (lane >> 5))
        left.append(jnp.where(column == 0, left_halo, lanes(cells, 1)))
        right.append(jnp.where(column == 31, right_halo, lanes(cells, -1)))
    return up, down, left, right


def coef_kernel(count_ref, kl_ref, cells_ref, coefs_ref, klq_ref, source, tiles):
    me = lax.axis_index("mode")
    mr, ml = me // 4, me % 4
    count = count_ref[0]
    source[0:13, :] = kl_ref[...]
    source[13:16, :] = jnp.zeros((3, 4096), F32)
    pack_tiles(source, 16, tiles, jnp.zeros((16, 128), F32))
    cells = cells_ref[...]
    faces = pick_faces(source, 16, cells >> 7, cells & 127)
    own = jnp.zeros((16, 128), F32)
    for s in range(4):
        for q in range(4):
            own = jnp.where(me == 4 * s + q, lanes(faces[s], -32 * q), own)
    klq_ref[...] = own
    lane = lane_ids(16)
    a = [tiles[me, :, group_of(v)] for v in range(3)]
    around = neighbours(*a)
    for v in range(2):
        row = 8 * mr + 4 * v + (lane >> 5)
        column = 32 * ml + (lane & 31)
        cell = 128 * row + column
        here = cell < count
        there = (
            (row > 0) & (cell - 128 < count),
            (row < 31) & (cell + 128 < count),
            (column > 0) & (cell - 1 < count),
            (column < 127) & (cell + 1 < count),
        )
        for d in range(4):
            value = 0.5 * (a[v] + around[d][v])
            coefs_ref[d, :, group_of(v)] = jnp.where(here & there[d], value, 0.0)


def face_rows(field_ref, s):
    low = field_ref[s, 24:32, group_of(0)]
    sub = lax.broadcasted_iota(jnp.int32, (8, 128), 0)
    return jnp.where(sub < 4, pltpu.roll(low, 4, 0), field_ref[s, 24:32, group_of(1)])


def outgoing_kernel(field_ref, klq_ref, out_ref):
    for s in range(PARTS):
        out_ref[8 * s : 8 * s + 8, :] = face_rows(field_ref, s)
    out_ref[128:144, :] = klq_ref[...]


def apply_kernel(field_ref, coefs_ref, total, hi_ref, lo_ref, steps, table, w_hi, w_lo):
    for s in range(PARTS):
        rows = pl.ds(HERE * s, HERE)
        cells = [field_ref[s, 0:HERE, group_of(v)] for v in range(3)]
        around = neighbours(*cells)
        for d in range(4):
            for v in range(2):
                steps[d, rows, group_of(v)] = cells[v] - around[d][v]
        table[rows, :] = cells[2]

    def stencil(k, rows):
        w = coefs_ref[0, k : k + 1, :] * steps[0, rows, :]
        for d in range(1, 4):
            w = w + coefs_ref[d, k : k + 1, :] * steps[d, rows, :]
        return w

    lane = lax.broadcasted_iota(jnp.int16, (16, 128), 1)
    nothing = jnp.zeros((16, 128), BF16)

    def mix(k):
        for c in range(MODES // 16):
            rows = pl.ds(16 * c, 16)
            entry = table[rows, :]
            wide = []
            for kk in (k, k + 1):
                cols = [entry[:, 80 + 12 * t + kk : 81 + 12 * t + kk] for t in range(4)]
                high = [col.astype(BF16) for col in cols[2:]]
                low = [(col - h.astype(F32)).astype(BF16) for col, h in zip(cols[2:], high)]
                modes = [col.astype(jnp.int32).astype(jnp.int16) for col in cols[:2]]
                wide.append([jnp.broadcast_to(part, (16, 128)) for part in modes + high + low])
            for g in range(7):
                if g < 3:
                    first, second, h0, h1, l0, l1 = wide[0]
                    at = lane + jnp.int16(128 * g)
                elif g == 3:
                    first, second, h0, h1, l0, l1 = (jnp.where(lane < 64, a, b) for a, b in zip(*wide))
                    at = jnp.where(lane < 64, lane + jnp.int16(384), lane - jnp.int16(64))
                else:
                    first, second, h0, h1, l0, l1 = wide[1]
                    at = lane + jnp.int16(128 * g - MODES)
                first, second = first == at, second == at
                to = pl.ds(MODES * k + 128 * g, 128)
                hi_ref[rows, to] = jnp.where(first, h0, jnp.where(second, h1, nothing))
                lo_ref[rows, to] = jnp.where(first, l0, jnp.where(second, l1, nothing))

    def prepare(pair):
        mix(2 * pair)
        for b in range(14 * pair, 14 * pair + 14):
            w = stencil(b // 7 + 1, pl.ds(64 * (b % 7), 64))
            high = w.astype(BF16)
            w_hi[64 * b : 64 * b + 64, :] = high
            w_lo[64 * b : 64 * b + 64, :] = (w - high.astype(F32)).astype(BF16)

    for b in range(7):
        rows = pl.ds(64 * b, 64)
        total[rows, :] = stencil(0, rows)
    prepare(0)
    for c in range(DEPTH // CHUNK):
        if c + 1 < TERMS // 2:
            prepare(c + 1)
        at = pl.ds(c * CHUNK, CHUNK)
        dot = lambda x, y: jnp.dot(x[:, at], y[at, :], preferred_element_type=F32)
        total[...] += dot(hi_ref, w_hi) + dot(hi_ref, w_lo) + dot(lo_ref, w_hi)


def flux_kernel(
    faces_ref, field_ref, remote_ref, klq_ref, main_ref, hi_ref, lo_ref, out_ref, steps, coefs, values, total
):
    me = lax.axis_index("mode")
    lane = lane_ids(16)
    live = (lane < 32) & (32 * (me % 4) + lane < faces_ref[me // 4])
    coefs[...] = jnp.where(live, 0.5 * (klq_ref[...] + remote_ref[128:144, :]), 0.0)
    first = lane_ids(8) < 32
    for s in range(PARTS):
        packed = face_rows(field_ref, s) - remote_ref[8 * s : 8 * s + 8, :]
        for u in range(7):
            piece = jnp.where(first, lanes(packed, -32 * (u % 4)), 0.0)
            row = HERE * s + 4 * u
            steps[row : row + 4, :] = piece[4 * (u // 4) : 4 * (u // 4) + 4]
    total[...] = coefs[0:1, :] * steps[...]
    for k in range(TERMS):
        w = coefs[k + 1 : k + 2, :] * steps[...]
        high = w.astype(BF16).astype(F32)
        values[MODES * k : MODES * k + MODES, :] = (high + lanes(w - high, 32)).astype(BF16)
    for c in range(DEPTH // CHUNK):
        at = pl.ds(c * CHUNK, CHUNK)
        dot = lambda x: jnp.dot(x[:, at], values[at, :], preferred_element_type=F32)
        total[...] += dot(hi_ref) + dot(lo_ref)
    total[...] = total[...] + lanes(total[...], 96)
    group = lane_ids(4) >> 5
    for s in range(PARTS):
        out_ref[s, 0:HERE, :] = main_ref[HERE * s : HERE * s + HERE, :]
        for v in range(2):
            packed = jnp.zeros((4, 128), F32)
            for u in range(4 * v, min(4 * v + 4, 7)):
                flux = total[HERE * s + 4 * u : HERE * s + 4 * u + 4, :]
                packed = jnp.where(group == u % 4, lanes(flux, 32 * (u % 4)), packed)
            out_ref[s, HERE:32, group_of(v)] = packed


def unpack_kernel(count_ref, tiles_ref, cells_ref, out_ref, flux, left_hi, left_lo, added):
    count = count_ref[0]
    sub = lax.broadcasted_iota(jnp.int32, (8, 128), 0)
    group = lane_ids(8) >> 5
    for s in range(4):
        for tau in range(4):
            value = jnp.zeros((8, 128), F32)
            for q in range(4):
                low = tiles_ref[4 * s + q, 24:32, group_of(tau // 2)]
                even = pltpu.roll(lanes(low, 32 * (q - (2 * tau) % 4)), 4, 0)
                odd = lanes(low, 32 * (q - (2 * tau + 1) % 4))
                value = jnp.where(group == q, jnp.where(sub < 4, even, odd), value)
            if tau == 3:
                value = jnp.where(sub < 4, value, 0.0)
            flux[8 * tau : 8 * tau + 8, group_of(s)] = value
    face_row = [cells_ref[s : s + 1, :] >> 7 for s in range(4)]
    high = [flux[:, group_of(s)].astype(BF16).astype(F32) for s in range(4)]
    low = [flux[:, group_of(s)] - high[s] for s in range(4)]
    for r in range(32):
        for s in range(4):
            at = (pl.ds(32 * r, 32), group_of(s))
            left_hi[at] = jnp.where(face_row[s] == r, high[s], 0.0).astype(BF16)
            left_lo[at] = jnp.where(face_row[s] == r, low[s], 0.0).astype(BF16)
    column = lax.broadcasted_iota(jnp.int32, (128, 128), 0)
    pick = jnp.concatenate(
        [jnp.where((cells_ref[s : s + 1, :] & 127) == column, 1.0, 0.0) for s in range(4)], axis=1
    ).astype(BF16)
    spread = lambda x: lax.dot_general(x[...], pick, (((1,), (1,)), ((), ())), preferred_element_type=F32)
    added[...] = spread(left_hi) + spread(left_lo)
    lane = lane_ids(32)
    group = lane >> 5
    for mr in range(4):
        for v in range(2):
            tiles = [tiles_ref[4 * mr + ml, :, group_of(v)] for ml in range(4)]
            for j in range(4):
                row = 8 * mr + 4 * v + j
                value = lanes(tiles[0], -32 * j)
                for ml in range(1, 4):
                    value = jnp.where(group == ml, lanes(tiles[ml], 32 * (ml - j)), value)
                value = value + added[32 * row : 32 * row + 32, :]
                value = jnp.where(lane + 128 * row < count, value, 0.0)
                out_ref[:, group_of(row)] = value[0:HERE]


def face_route(blocks):
    route = []
    for b in range(blocks):
        for s, offset in enumerate(SLOT_OFFSETS):
            if 0 <= b + offset < blocks:
                for q in range(4):
                    route.append((16 * b + 4 * s + q, 16 * (b + offset) + 4 * (3 - s) + q))
    return route


VMEM = pl.BlockSpec(memory_space=pltpu.VMEM)
SMEM = pl.BlockSpec(memory_space=pltpu.SMEM)
HBM = pl.BlockSpec(memory_space=pltpu.HBM)


def kernel_call(body, name, shapes, in_specs, scratch, micros, limit):
    return pl.pallas_call(
        body,
        out_shape=shapes,
        in_specs=in_specs,
        out_specs=tuple(VMEM for _ in shapes) if isinstance(shapes, tuple) else VMEM,
        scratch_shapes=scratch,
        compiler_params=pltpu.CompilerParams(vmem_limit_bytes=limit << 20),
        cost_estimate=pl.CostEstimate(flops=int(micros * 1e9), bytes_accessed=int(micros * 1e6), transcendentals=0),
        name=name,
    )


def array(*shape):
    return jax.ShapeDtypeStruct(shape, F32)


def per_device(chaos_field, kl_field, partner, chaos_coef, cell_count, face_count, face_cells):
    cells = face_cells[0]
    send = kernel_call(
        pack_kernel,
        "pack",
        array(PARTS, 32, 384),
        [SMEM, HBM, VMEM, HBM, HBM],
        [
            pltpu.VMEM((HERE, 4096), F32),
            pltpu.VMEM(partner.shape, jnp.int32),
            pltpu.VMEM(chaos_coef.shape, F32),
            pltpu.VMEM((128, 128), F32),
            pltpu.SemaphoreType.DMA((3,)),
        ],
        4,
        58,
    )(cell_count, chaos_field, cells, partner, chaos_coef)
    field = lax.all_to_all(send, "mode", 0, 0, tiled=True)
    coefs, klq = kernel_call(
        coef_kernel,
        "coefs",
        (array(4, 16, 256), array(16, 128)),
        [SMEM, VMEM, VMEM],
        [pltpu.VMEM((16, 4096), F32), pltpu.VMEM((PARTS, 16, 384), F32)],
        2,
        8,
    )(cell_count, kl_field, cells)
    outgoing = kernel_call(outgoing_kernel, "outgoing", array(144, 128), [VMEM] * 2, [], 0.5, 4)(field, klq)
    remote = lax.ppermute(outgoing, ("blk", "mode"), face_route(lax.axis_size("blk")))
    mix = jax.ShapeDtypeStruct((MODES, DEPTH), BF16)
    main, mix_hi, mix_lo = kernel_call(
        apply_kernel,
        "apply",
        (array(MODES, 256), mix, mix),
        [VMEM] * 2,
        [
            pltpu.VMEM((4, MODES, 256), F32),
            pltpu.VMEM((MODES, 128), F32),
            pltpu.VMEM((DEPTH, 256), BF16),
            pltpu.VMEM((DEPTH, 256), BF16),
        ],
        8,
        24,
    )(field, coefs)
    tiles = kernel_call(
        flux_kernel,
        "flux",
        array(PARTS, 32, 256),
        [SMEM] + [VMEM] * 6,
        [
            pltpu.VMEM((MODES, 128), F32),
            pltpu.VMEM((16, 128), F32),
            pltpu.VMEM((DEPTH, 128), BF16),
            pltpu.VMEM((MODES, 128), F32),
        ],
        4,
        8,
    )(face_count[0], field, remote, klq, main, mix_hi, mix_lo)
    back = lax.all_to_all(tiles, "mode", 0, 0, tiled=True)
    return kernel_call(
        unpack_kernel,
        "unpack",
        jax.ShapeDtypeStruct(chaos_field.shape, F32),
        [SMEM, VMEM, VMEM],
        [
            pltpu.VMEM((32, 512), F32),
            pltpu.VMEM((1024, 512), BF16),
            pltpu.VMEM((1024, 512), BF16),
            pltpu.VMEM((1024, 128), F32),
        ],
        3,
        8,
    )(cell_count, back, cells)


def solution(mesh):
    in_specs = (
        P("mode", "blk"),
        P(None, "blk"),
        P(None, None, "mode"),
        P(None, None, "mode"),
        P("blk"),
        P("blk", None),
        P("blk", None, None),
    )
    return jax.shard_map(
        per_device, mesh=mesh, in_specs=in_specs, out_specs=P("mode", "blk"), check_vma=False
    )
```

```python
import jax
import jax.numpy as jnp
from jax import lax
from jax.experimental import pallas as pl
from jax.experimental.pallas import tpu as pltpu
from jax.sharding import PartitionSpec as P

SLOT_OFFSETS = (-2, -1, 1, 2)
FACE_PLACE = (0, 2, 3, 1)
F32 = jnp.float32
BF16 = jnp.bfloat16
TERMS = 12
MODES = 448
PARTS = 16
HERE = MODES // PARTS
DEPTH = TERMS * MODES
CHUNK = 768


def lanes(value, shift):
    shift = shift % 128
    return value if shift == 0 else pltpu.roll(value, shift, 1)


def lane_ids(rows):
    return lax.broadcasted_iota(jnp.int32, (rows, 128), 1)


def along(value, index):
    return jnp.take_along_axis(value, index, axis=1, mode="promise_in_bounds")


def group_of(v):
    return pl.ds(128 * v, 128)


def pick_faces(source, rows, face_row, face_lane):
    faces = [jnp.zeros((rows, 128), F32) for _ in range(4)]
    picks = [jnp.broadcast_to(face_lane[s : s + 1], (rows, 128)) for s in range(4)]
    for r in range(32):
        cells = source[:, group_of(r)]
        for s in range(4):
            faces[s] = jnp.where(face_row[s : s + 1] == r, along(cells, picks[s]), faces[s])
    return faces


def pack_rows(load, rows, mr, out_ref):
    group = lane_ids(rows) >> 5
    for v in range(2):
        cells = [load(8 * mr + 4 * v + j) for j in range(4)]
        for ml in range(4):
            tile = lanes(cells[0], -32 * ml)
            for j in range(1, 4):
                tile = jnp.where(group == j, lanes(cells[j], 32 * (j - ml)), tile)
            out_ref[4 * mr + ml, 0:rows, group_of(v)] = tile


def pack_halo(rows, m, out_ref, table):
    lane = lane_ids(rows)
    left_pick = jnp.where((lane >= 64) & (lane < 72), 32 * (lane & 3) + 31, 0)
    right_pick = jnp.where((lane >= 72) & (lane < 80), 32 * (lane & 3), 0)
    halo = table
    if m >= 4:
        halo = jnp.where(lane < 32, lanes(out_ref[m - 4, 0:rows, group_of(1)], 32), halo)
    if m < 12:
        below = lanes(out_ref[m + 4, 0:rows, group_of(0)], 32)
        halo = jnp.where((lane >= 32) & (lane < 64), below, halo)
    for v in range(2):
        if m % 4 > 0:
            side = along(out_ref[m - 1, 0:rows, group_of(v)], left_pick)
            halo = jnp.where((lane >= 64 + 4 * v) & (lane < 68 + 4 * v), side, halo)
        if m % 4 < 3:
            side = along(out_ref[m + 1, 0:rows, group_of(v)], right_pick)
            halo = jnp.where((lane >= 72 + 4 * v) & (lane < 76 + 4 * v), side, halo)
    out_ref[m, 0:rows, group_of(2)] = halo


def pack_kernel(
    count_ref, far_field, cells_ref, far_partner, far_coef, far_send,
    field_ref, partner_ref, coef_ref, stage, send_ref, arrived, left,
):
    copies = [
        pltpu.make_async_copy(far_partner, partner_ref, arrived.at[4]),
        pltpu.make_async_copy(far_coef, coef_ref, arrived.at[5]),
    ]
    blocks = [
        pltpu.make_async_copy(far_field.at[:, pl.ds(1024 * i, 1024)], field_ref.at[:, pl.ds(1024 * i, 1024)], arrived.at[i])
        for i in range(4)
    ]
    for copy in copies + blocks:
        copy.start()
    stage[...] = jnp.zeros((128, 128), F32)
    for copy in copies:
        copy.wait()
    for k in range(TERMS):
        mode, coef = partner_ref[k], coef_ref[k]
        same = mode[0:1] == mode[1:2]
        stage[80 + k : 81 + k, 0:HERE] = mode[0:1].astype(F32)
        stage[92 + k : 93 + k, 0:HERE] = mode[1:2].astype(F32)
        stage[104 + k : 105 + k, 0:HERE] = coef[0:1] + jnp.where(same, coef[1:2], 0.0)
        stage[116 + k : 117 + k, 0:HERE] = coef[1:2]
    table = stage[...].T[0:HERE]
    count = count_ref[0]
    lane = lane_ids(HERE)
    cells = cells_ref[...]
    faces = [jnp.zeros((HERE, 128), F32) for _ in range(4)]
    picks = [jnp.broadcast_to(cells[s : s + 1] & 127, (HERE, 128)) for s in range(4)]
    live = lambda r: jnp.where(lane + 128 * r < count, field_ref[:, group_of(r)], 0.0)
    for mr in range(4):
        blocks[mr].wait()
        for r in range(8 * mr, 8 * mr + 8):
            row = live(r)
            for s in range(4):
                faces[s] = jnp.where(cells[s : s + 1] >> 7 == r, along(row, picks[s]), faces[s])
        pack_rows(live, HERE, mr, send_ref)
    group = lane_ids(4) >> 5
    for s in range(4):
        turned = [lanes(faces[s], 32 * t) for t in range(4)]
        for q in range(4):
            m = 4 * q + FACE_PLACE[s]
            for v in range(2):
                packed = jnp.zeros((4, 128), F32)
                for u in range(4 * v, min(4 * v + 4, 7)):
                    packed = jnp.where(group == u % 4, turned[(u - q) % 4][4 * u : 4 * u + 4], packed)
                send_ref[m, HERE:32, group_of(v)] = packed
            send_ref[m, HERE:32, group_of(2)] = jnp.zeros((4, 128), F32)
    copies = []
    for m in range(PARTS):
        pack_halo(HERE, m, send_ref, table)
        copies.append(pltpu.make_async_copy(send_ref.at[m], far_send.at[m], left.at[m]))
        copies[m].start()
    for copy in copies:
        copy.wait()


def neighbours(first, second, halo):
    rows = first.shape[0]
    lane = lane_ids(rows)
    up_first, up_second = lanes(first, 32), lanes(second, 32)
    down_first, down_second = lanes(first, -32), lanes(second, -32)
    up = (jnp.where(lane < 32, halo, up_first), jnp.where(lane < 32, up_first, up_second))
    down = (jnp.where(lane < 96, down_first, down_second), jnp.where(lane < 96, down_second, lanes(halo, 64)))
    column = lane & 31
    left, right = [], []
    for v, cells in enumerate((first, second)):
        left_halo = along(halo, 64 + 4 * v + (lane >> 5))
        right_halo = along(halo, 72 + 4 * v + (lane >> 5))
        left.append(jnp.where(column == 0, left_halo, lanes(cells, 1)))
        right.append(jnp.where(column == 31, right_halo, lanes(cells, -1)))
    return up, down, left, right


def coef_kernel(count_ref, kl_ref, cells_ref, coefs_ref, klq_ref, source, tiles):
    me = lax.axis_index("mode")
    mr, ml = me // 4, me % 4
    count = count_ref[0]
    source[0:13, :] = kl_ref[...]
    source[13:16, :] = jnp.zeros((3, 4096), F32)
    for part in range(4):
        pack_rows(lambda r: source[:, group_of(r)], 16, part, tiles)
    for m in range(PARTS):
        pack_halo(16, m, tiles, jnp.zeros((16, 128), F32))
    cells = cells_ref[...]
    faces = pick_faces(source, 16, cells >> 7, cells & 127)
    own = jnp.zeros((16, 128), F32)
    for s in range(4):
        for q in range(4):
            own = jnp.where(me == 4 * q + FACE_PLACE[s], lanes(faces[s], -32 * q), own)
    klq_ref[...] = own
    lane = lane_ids(16)
    a = [tiles[me, :, group_of(v)] for v in range(3)]
    around = neighbours(*a)
    for v in range(2):
        row = 8 * mr + 4 * v + (lane >> 5)
        column = 32 * ml + (lane & 31)
        cell = 128 * row + column
        here = cell < count
        there = (
            (row > 0) & (cell - 128 < count),
            (row < 31) & (cell + 128 < count),
            (column > 0) & (cell - 1 < count),
            (column < 127) & (cell + 1 < count),
        )
        for d in range(4):
            value = 0.5 * (a[v] + around[d][v])
            coefs_ref[d, :, group_of(v)] = jnp.where(here & there[d], value, 0.0)


def face_rows(field_ref, s):
    low = field_ref[s, 24:32, group_of(0)]
    sub = lax.broadcasted_iota(jnp.int32, (8, 128), 0)
    return jnp.where(sub < 4, pltpu.roll(low, 4, 0), field_ref[s, 24:32, group_of(1)])


def outgoing_kernel(field_ref, klq_ref, out_ref):
    for s in range(PARTS):
        out_ref[8 * s : 8 * s + 8, :] = face_rows(field_ref, s)
    out_ref[128:144, :] = klq_ref[...]


def apply_kernel(field_ref, coefs_ref, total, hi_ref, lo_ref, steps, table, w_hi, w_lo):
    for s in range(PARTS):
        rows = pl.ds(HERE * s, HERE)
        cells = [field_ref[s, 0:HERE, group_of(v)] for v in range(3)]
        around = neighbours(*cells)
        for d in range(4):
            for v in range(2):
                steps[d, rows, group_of(v)] = cells[v] - around[d][v]
        table[rows, :] = cells[2]

    def stencil(k, rows):
        w = coefs_ref[0, k : k + 1, :] * steps[0, rows, :]
        for d in range(1, 4):
            w = w + coefs_ref[d, k : k + 1, :] * steps[d, rows, :]
        return w

    lane = lax.broadcasted_iota(jnp.int16, (16, 128), 1)
    nothing = jnp.zeros((16, 128), BF16)

    def mix(k):
        for c in range(MODES // 16):
            rows = pl.ds(16 * c, 16)
            entry = table[rows, :]
            wide = []
            for kk in (k, k + 1):
                cols = [entry[:, 80 + 12 * t + kk : 81 + 12 * t + kk] for t in range(4)]
                high = [col.astype(BF16) for col in cols[2:]]
                low = [(col - h.astype(F32)).astype(BF16) for col, h in zip(cols[2:], high)]
                modes = [col.astype(jnp.int32).astype(jnp.int16) for col in cols[:2]]
                wide.append([jnp.broadcast_to(part, (16, 128)) for part in modes + high + low])
            for g in range(7):
                if g < 3:
                    first, second, h0, h1, l0, l1 = wide[0]
                    at = lane + jnp.int16(128 * g)
                elif g == 3:
                    first, second, h0, h1, l0, l1 = (jnp.where(lane < 64, a, b) for a, b in zip(*wide))
                    at = jnp.where(lane < 64, lane + jnp.int16(384), lane - jnp.int16(64))
                else:
                    first, second, h0, h1, l0, l1 = wide[1]
                    at = lane + jnp.int16(128 * g - MODES)
                first, second = first == at, second == at
                to = pl.ds(MODES * k + 128 * g, 128)
                hi_ref[rows, to] = jnp.where(first, h0, jnp.where(second, h1, nothing))
                lo_ref[rows, to] = jnp.where(first, l0, jnp.where(second, l1, nothing))

    def prepare(pair):
        mix(2 * pair)
        for b in range(14 * pair, 14 * pair + 14):
            w = stencil(b // 7 + 1, pl.ds(64 * (b % 7), 64))
            high = w.astype(BF16)
            w_hi[64 * b : 64 * b + 64, :] = high
            w_lo[64 * b : 64 * b + 64, :] = (w - high.astype(F32)).astype(BF16)

    for b in range(7):
        rows = pl.ds(64 * b, 64)
        total[rows, :] = stencil(0, rows)
    prepare(0)
    for c in range(DEPTH // CHUNK):
        if c + 1 < TERMS // 2:
            prepare(c + 1)
        at = pl.ds(c * CHUNK, CHUNK)
        dot = lambda x, y: jnp.dot(x[:, at], y[at, :], preferred_element_type=F32)
        total[...] += dot(hi_ref, w_hi) + dot(hi_ref, w_lo) + dot(lo_ref, w_hi)


def flux_kernel(
    faces_ref, field_ref, remote_ref, klq_ref, main_ref, hi_ref, lo_ref, out_ref, steps, coefs, values, total
):
    me = lax.axis_index("mode")
    lane = lane_ids(16)
    limit = faces_ref[0]
    for s in range(1, 4):
        limit = jnp.where(me % 4 == FACE_PLACE[s], faces_ref[s], limit)
    live = (lane < 32) & (32 * (me // 4) + lane < limit)
    coefs[...] = jnp.where(live, 0.5 * (klq_ref[...] + remote_ref[128:144, :]), 0.0)
    first = lane_ids(8) < 32
    for s in range(PARTS):
        packed = face_rows(field_ref, s) - remote_ref[8 * s : 8 * s + 8, :]
        for u in range(7):
            piece = jnp.where(first, lanes(packed, -32 * (u % 4)), 0.0)
            row = HERE * s + 4 * u
            steps[row : row + 4, :] = piece[4 * (u // 4) : 4 * (u // 4) + 4]
    total[...] = coefs[0:1, :] * steps[...]
    for k in range(TERMS):
        w = coefs[k + 1 : k + 2, :] * steps[...]
        high = w.astype(BF16).astype(F32)
        values[MODES * k : MODES * k + MODES, :] = (high + lanes(w - high, 32)).astype(BF16)
    for c in range(DEPTH // CHUNK):
        at = pl.ds(c * CHUNK, CHUNK)
        dot = lambda x: jnp.dot(x[:, at], values[at, :], preferred_element_type=F32)
        total[...] += dot(hi_ref) + dot(lo_ref)
    total[...] = total[...] + lanes(total[...], 96)
    group = lane_ids(4) >> 5
    for s in range(PARTS):
        out_ref[s, 0:HERE, :] = main_ref[HERE * s : HERE * s + HERE, :]
        for v in range(2):
            packed = jnp.zeros((4, 128), F32)
            for u in range(4 * v, min(4 * v + 4, 7)):
                flux = total[HERE * s + 4 * u : HERE * s + 4 * u + 4, :]
                packed = jnp.where(group == u % 4, lanes(flux, 32 * (u % 4)), packed)
            out_ref[s, HERE:32, group_of(v)] = packed


def unpack_kernel(count_ref, tiles_ref, cells_ref, far_out, flux, left_hi, left_lo, added, out_ref, left):
    copies = []
    count = count_ref[0]
    sub = lax.broadcasted_iota(jnp.int32, (8, 128), 0)
    group = lane_ids(8) >> 5
    for s in range(4):
        for tau in range(4):
            value = jnp.zeros((8, 128), F32)
            for q in range(4):
                low = tiles_ref[4 * q + FACE_PLACE[s], 24:32, group_of(tau // 2)]
                even = pltpu.roll(lanes(low, 32 * (q - (2 * tau) % 4)), 4, 0)
                odd = lanes(low, 32 * (q - (2 * tau + 1) % 4))
                value = jnp.where(group == q, jnp.where(sub < 4, even, odd), value)
            if tau == 3:
                value = jnp.where(sub < 4, value, 0.0)
            flux[8 * tau : 8 * tau + 8, group_of(s)] = value
    face_row = [cells_ref[s : s + 1, :] >> 7 for s in range(4)]
    high = [flux[:, group_of(s)].astype(BF16).astype(F32) for s in range(4)]
    low = [flux[:, group_of(s)] - high[s] for s in range(4)]
    for r in range(32):
        for s in range(4):
            at = (pl.ds(32 * r, 32), group_of(s))
            left_hi[at] = jnp.where(face_row[s] == r, high[s], 0.0).astype(BF16)
            left_lo[at] = jnp.where(face_row[s] == r, low[s], 0.0).astype(BF16)
    column = lax.broadcasted_iota(jnp.int32, (128, 128), 0)
    pick = jnp.concatenate(
        [jnp.where((cells_ref[s : s + 1, :] & 127) == column, 1.0, 0.0) for s in range(4)], axis=1
    ).astype(BF16)
    spread = lambda x: lax.dot_general(x[...], pick, (((1,), (1,)), ((), ())), preferred_element_type=F32)
    added[...] = spread(left_hi) + spread(left_lo)
    lane = lane_ids(32)
    group = lane >> 5
    for mr in range(4):
        for v in range(2):
            tiles = [tiles_ref[4 * mr + ml, :, group_of(v)] for ml in range(4)]
            for j in range(4):
                row = 8 * mr + 4 * v + j
                value = lanes(tiles[0], -32 * j)
                for ml in range(1, 4):
                    value = jnp.where(group == ml, lanes(tiles[ml], 32 * (ml - j)), value)
                value = value + added[32 * row : 32 * row + 32, :]
                value = jnp.where(lane + 128 * row < count, value, 0.0)
                out_ref[:, group_of(row)] = value[0:HERE]
        at = pl.ds(1024 * mr, 1024)
        copies.append(pltpu.make_async_copy(out_ref.at[:, at], far_out.at[:, at], left.at[mr]))
        copies[mr].start()
    for copy in copies:
        copy.wait()


def face_route(blocks):
    route = []
    for b in range(blocks):
        for s, offset in enumerate(SLOT_OFFSETS):
            if 0 <= b + offset < blocks:
                for q in range(4):
                    source, target = 4 * q + FACE_PLACE[s], 4 * q + FACE_PLACE[3 - s]
                    route.append((16 * b + source, 16 * (b + offset) + target))
    return route


VMEM = pl.BlockSpec(memory_space=pltpu.VMEM)
SMEM = pl.BlockSpec(memory_space=pltpu.SMEM)
HBM = pl.BlockSpec(memory_space=pl.ANY)


def kernel_call(body, name, shapes, in_specs, scratch, micros, limit, place=None):
    return pl.pallas_call(
        body,
        out_shape=shapes,
        in_specs=in_specs,
        out_specs=tuple(VMEM for _ in shapes) if isinstance(shapes, tuple) else place or VMEM,
        scratch_shapes=scratch,
        compiler_params=pltpu.CompilerParams(vmem_limit_bytes=limit << 20),
        cost_estimate=pl.CostEstimate(flops=int(micros * 1e9), bytes_accessed=int(micros * 1e6), transcendentals=0),
        name=name,
    )


def array(*shape):
    return jax.ShapeDtypeStruct(shape, F32)


def per_device(chaos_field, kl_field, partner, chaos_coef, cell_count, face_count, face_cells):
    cells = face_cells[0]
    send = kernel_call(
        pack_kernel,
        "pack",
        array(PARTS, 32, 384),
        [SMEM, HBM, VMEM, HBM, HBM],
        [
            pltpu.VMEM((HERE, 4096), F32),
            pltpu.VMEM(partner.shape, jnp.int32),
            pltpu.VMEM(chaos_coef.shape, F32),
            pltpu.VMEM((128, 128), F32),
            pltpu.VMEM((PARTS, 32, 384), F32),
            pltpu.SemaphoreType.DMA((6,)),
            pltpu.SemaphoreType.DMA((PARTS,)),
        ],
        4,
        58,
        HBM,
    )(cell_count, chaos_field, cells, partner, chaos_coef)
    field = lax.all_to_all(send, "mode", 0, 0, tiled=True)
    coefs, klq = kernel_call(
        coef_kernel,
        "coefs",
        (array(4, 16, 256), array(16, 128)),
        [SMEM, VMEM, VMEM],
        [pltpu.VMEM((16, 4096), F32), pltpu.VMEM((PARTS, 16, 384), F32)],
        2,
        8,
    )(cell_count, kl_field, cells)
    outgoing = kernel_call(outgoing_kernel, "outgoing", array(144, 128), [VMEM] * 2, [], 0.5, 4)(field, klq)
    remote = lax.ppermute(outgoing, ("blk", "mode"), face_route(lax.axis_size("blk")))
    mix = jax.ShapeDtypeStruct((MODES, DEPTH), BF16)
    main, mix_hi, mix_lo = kernel_call(
        apply_kernel,
        "apply",
        (array(MODES, 256), mix, mix),
        [VMEM] * 2,
        [
            pltpu.VMEM((4, MODES, 256), F32),
            pltpu.VMEM((MODES, 128), F32),
            pltpu.VMEM((DEPTH, 256), BF16),
            pltpu.VMEM((DEPTH, 256), BF16),
        ],
        8,
        24,
    )(field, coefs)
    tiles = kernel_call(
        flux_kernel,
        "flux",
        array(PARTS, 32, 256),
        [SMEM] + [VMEM] * 6,
        [
            pltpu.VMEM((MODES, 128), F32),
            pltpu.VMEM((16, 128), F32),
            pltpu.VMEM((DEPTH, 128), BF16),
            pltpu.VMEM((MODES, 128), F32),
        ],
        4,
        8,
    )(face_count[0], field, remote, klq, main, mix_hi, mix_lo)
    back = lax.all_to_all(tiles, "mode", 0, 0, tiled=True)
    return kernel_call(
        unpack_kernel,
        "unpack",
        jax.ShapeDtypeStruct(chaos_field.shape, F32),
        [SMEM, VMEM, VMEM],
        [
            pltpu.VMEM((32, 512), F32),
            pltpu.VMEM((1024, 512), BF16),
            pltpu.VMEM((1024, 512), BF16),
            pltpu.VMEM((1024, 128), F32),
            pltpu.VMEM((HERE, 4096), F32),
            pltpu.SemaphoreType.DMA((4,)),
        ],
        3,
        8,
        HBM,
    )(cell_count, back, cells)


def solution(mesh):
    in_specs = (
        P("mode", "blk"),
        P(None, "blk"),
        P(None, None, "mode"),
        P(None, None, "mode"),
        P("blk"),
        P("blk", None),
        P("blk", None, None),
    )
    return jax.shard_map(
        per_device, mesh=mesh, in_specs=in_specs, out_specs=P("mode", "blk"), check_vma=False
    )
```

```python
import jax
import jax.numpy as jnp
from jax import lax
from jax.experimental import pallas as pl
from jax.experimental.pallas import tpu as pltpu
from jax.sharding import PartitionSpec as P

SLOT_OFFSETS = (-2, -1, 1, 2)
FACE_PLACE = (0, 2, 3, 1)
F32 = jnp.float32
BF16 = jnp.bfloat16
TERMS = 12
MODES = 448
PARTS = 16
HERE = MODES // PARTS
DEPTH = TERMS * MODES
CHUNK = 768


def lanes(value, shift):
    shift = shift % 128
    return value if shift == 0 else pltpu.roll(value, shift, 1)


def lane_ids(rows):
    return lax.broadcasted_iota(jnp.int32, (rows, 128), 1)


def along(value, index):
    return jnp.take_along_axis(value, index, axis=1, mode="promise_in_bounds")


def group_of(v):
    return pl.ds(128 * v, 128)


def pick_faces(source, rows, face_row, face_lane):
    faces = [jnp.zeros((rows, 128), F32) for _ in range(4)]
    picks = [jnp.broadcast_to(face_lane[s : s + 1], (rows, 128)) for s in range(4)]
    for r in range(32):
        cells = source[:, group_of(r)]
        for s in range(4):
            faces[s] = jnp.where(face_row[s : s + 1] == r, along(cells, picks[s]), faces[s])
    return faces


def pack_rows(load, rows, mr, out_ref):
    group = lane_ids(rows) >> 5
    for v in range(2):
        cells = [load(8 * mr + 4 * v + j) for j in range(4)]
        for ml in range(4):
            tile = lanes(cells[0], -32 * ml)
            for j in range(1, 4):
                tile = jnp.where(group == j, lanes(cells[j], 32 * (j - ml)), tile)
            out_ref[4 * mr + ml, 0:rows, group_of(v)] = tile


def pack_halo(rows, m, out_ref, table):
    lane = lane_ids(rows)
    left_pick = jnp.where((lane >= 64) & (lane < 72), 32 * (lane & 3) + 31, 0)
    right_pick = jnp.where((lane >= 72) & (lane < 80), 32 * (lane & 3), 0)
    halo = table
    if m >= 4:
        halo = jnp.where(lane < 32, lanes(out_ref[m - 4, 0:rows, group_of(1)], 32), halo)
    if m < 12:
        below = lanes(out_ref[m + 4, 0:rows, group_of(0)], 32)
        halo = jnp.where((lane >= 32) & (lane < 64), below, halo)
    for v in range(2):
        if m % 4 > 0:
            side = along(out_ref[m - 1, 0:rows, group_of(v)], left_pick)
            halo = jnp.where((lane >= 64 + 4 * v) & (lane < 68 + 4 * v), side, halo)
        if m % 4 < 3:
            side = along(out_ref[m + 1, 0:rows, group_of(v)], right_pick)
            halo = jnp.where((lane >= 72 + 4 * v) & (lane < 76 + 4 * v), side, halo)
    out_ref[m, 0:rows, group_of(2)] = halo


def pack_kernel(
    count_ref, far_field, far_kl, far_cells, far_partner, far_coef, send_ref, coefs_ref, klq_ref,
    cells_ref, field_ref, kl_ref, kl_pad, tiles, partner_ref, coef_ref, stage, arrived,
):
    copies = [
        pltpu.make_async_copy(far_partner, partner_ref, arrived.at[4]),
        pltpu.make_async_copy(far_coef, coef_ref, arrived.at[5]),
        pltpu.make_async_copy(far_cells, cells_ref, arrived.at[7]),
        pltpu.make_async_copy(far_kl, kl_ref, arrived.at[6]),
    ]
    blocks = [
        pltpu.make_async_copy(far_field.at[:, pl.ds(1024 * i, 1024)], field_ref.at[:, pl.ds(1024 * i, 1024)], arrived.at[i])
        for i in range(4)
    ]
    for copy in copies + blocks:
        copy.start()
    stage[...] = jnp.zeros((128, 128), F32)
    for copy in copies:
        copy.wait()
    for k in range(TERMS):
        mode, coef = partner_ref[k], coef_ref[k]
        same = mode[0:1] == mode[1:2]
        stage[80 + k : 81 + k, 0:HERE] = mode[0:1].astype(F32)
        stage[92 + k : 93 + k, 0:HERE] = mode[1:2].astype(F32)
        stage[104 + k : 105 + k, 0:HERE] = coef[0:1] + jnp.where(same, coef[1:2], 0.0)
        stage[116 + k : 117 + k, 0:HERE] = coef[1:2]
    table = stage[...].T[0:HERE]
    kl_pad[0:13, :] = kl_ref[...]
    kl_pad[13:16, :] = jnp.zeros((3, 4096), F32)
    face_coefficients(count_ref, cells_ref, coefs_ref, klq_ref, kl_pad, tiles)
    count = count_ref[0]
    lane = lane_ids(HERE)
    cells = cells_ref[...]
    faces = [jnp.zeros((HERE, 128), F32) for _ in range(4)]
    picks = [jnp.broadcast_to(cells[s : s + 1] & 127, (HERE, 128)) for s in range(4)]
    live = lambda r: jnp.where(lane + 128 * r < count, field_ref[:, group_of(r)], 0.0)
    for mr in range(4):
        blocks[mr].wait()
        for r in range(8 * mr, 8 * mr + 8):
            row = live(r)
            for s in range(4):
                faces[s] = jnp.where(cells[s : s + 1] >> 7 == r, along(row, picks[s]), faces[s])
        pack_rows(live, HERE, mr, send_ref)
    group = lane_ids(4) >> 5
    for s in range(4):
        turned = [lanes(faces[s], 32 * t) for t in range(4)]
        for q in range(4):
            m = 4 * q + FACE_PLACE[s]
            for v in range(2):
                packed = jnp.zeros((4, 128), F32)
                for u in range(4 * v, min(4 * v + 4, 7)):
                    packed = jnp.where(group == u % 4, turned[(u - q) % 4][4 * u : 4 * u + 4], packed)
                send_ref[m, HERE:32, group_of(v)] = packed
            send_ref[m, HERE:32, group_of(2)] = jnp.zeros((4, 128), F32)
    copies = []
    for m in range(PARTS):
        pack_halo(HERE, m, send_ref, table)


def neighbours(first, second, halo):
    rows = first.shape[0]
    lane = lane_ids(rows)
    up_first, up_second = lanes(first, 32), lanes(second, 32)
    down_first, down_second = lanes(first, -32), lanes(second, -32)
    up = (jnp.where(lane < 32, halo, up_first), jnp.where(lane < 32, up_first, up_second))
    down = (jnp.where(lane < 96, down_first, down_second), jnp.where(lane < 96, down_second, lanes(halo, 64)))
    column = lane & 31
    left, right = [], []
    for v, cells in enumerate((first, second)):
        left_halo = along(halo, 64 + 4 * v + (lane >> 5))
        right_halo = along(halo, 72 + 4 * v + (lane >> 5))
        left.append(jnp.where(column == 0, left_halo, lanes(cells, 1)))
        right.append(jnp.where(column == 31, right_halo, lanes(cells, -1)))
    return up, down, left, right


def face_coefficients(count_ref, cells_ref, coefs_ref, klq_ref, source, tiles):
    me = lax.axis_index("mode")
    mr, ml = me // 4, me % 4
    count = count_ref[0]
    for part in range(4):
        pack_rows(lambda r: source[:, group_of(r)], 16, part, tiles)
    for m in range(PARTS):
        pack_halo(16, m, tiles, jnp.zeros((16, 128), F32))
    cells = cells_ref[...]
    faces = pick_faces(source, 16, cells >> 7, cells & 127)
    own = jnp.zeros((16, 128), F32)
    for s in range(4):
        for q in range(4):
            own = jnp.where(me == 4 * q + FACE_PLACE[s], lanes(faces[s], -32 * q), own)
    klq_ref[...] = own
    lane = lane_ids(16)
    a = [tiles[me, :, group_of(v)] for v in range(3)]
    around = neighbours(*a)
    for v in range(2):
        row = 8 * mr + 4 * v + (lane >> 5)
        column = 32 * ml + (lane & 31)
        cell = 128 * row + column
        here = cell < count
        there = (
            (row > 0) & (cell - 128 < count),
            (row < 31) & (cell + 128 < count),
            (column > 0) & (cell - 1 < count),
            (column < 127) & (cell + 1 < count),
        )
        for d in range(4):
            value = 0.5 * (a[v] + around[d][v])
            coefs_ref[d, :, group_of(v)] = jnp.where(here & there[d], value, 0.0)


def face_rows(field_ref, s):
    low = field_ref[s, 24:32, group_of(0)]
    sub = lax.broadcasted_iota(jnp.int32, (8, 128), 0)
    return jnp.where(sub < 4, pltpu.roll(low, 4, 0), field_ref[s, 24:32, group_of(1)])


def outgoing_kernel(field_ref, klq_ref, out_ref):
    for s in range(PARTS):
        out_ref[8 * s : 8 * s + 8, :] = face_rows(field_ref, s)
    out_ref[128:144, :] = klq_ref[...]


def apply_kernel(field_ref, coefs_ref, total, hi_ref, lo_ref, steps, table, w_hi, w_lo):
    for s in range(PARTS):
        rows = pl.ds(HERE * s, HERE)
        cells = [field_ref[s, 0:HERE, group_of(v)] for v in range(3)]
        around = neighbours(*cells)
        for d in range(4):
            for v in range(2):
                steps[d, rows, group_of(v)] = cells[v] - around[d][v]
        table[rows, :] = cells[2]

    def stencil(k, rows):
        w = coefs_ref[0, k : k + 1, :] * steps[0, rows, :]
        for d in range(1, 4):
            w = w + coefs_ref[d, k : k + 1, :] * steps[d, rows, :]
        return w

    lane = lax.broadcasted_iota(jnp.int16, (16, 128), 1)
    nothing = jnp.zeros((16, 128), BF16)

    def mix(k):
        for c in range(MODES // 16):
            rows = pl.ds(16 * c, 16)
            entry = table[rows, :]
            wide = []
            for kk in (k, k + 1):
                cols = [entry[:, 80 + 12 * t + kk : 81 + 12 * t + kk] for t in range(4)]
                high = [col.astype(BF16) for col in cols[2:]]
                low = [(col - h.astype(F32)).astype(BF16) for col, h in zip(cols[2:], high)]
                modes = [col.astype(jnp.int32).astype(jnp.int16) for col in cols[:2]]
                wide.append([jnp.broadcast_to(part, (16, 128)) for part in modes + high + low])
            for g in range(7):
                if g < 3:
                    first, second, h0, h1, l0, l1 = wide[0]
                    at = lane + jnp.int16(128 * g)
                elif g == 3:
                    first, second, h0, h1, l0, l1 = (jnp.where(lane < 64, a, b) for a, b in zip(*wide))
                    at = jnp.where(lane < 64, lane + jnp.int16(384), lane - jnp.int16(64))
                else:
                    first, second, h0, h1, l0, l1 = wide[1]
                    at = lane + jnp.int16(128 * g - MODES)
                first, second = first == at, second == at
                to = pl.ds(MODES * k + 128 * g, 128)
                hi_ref[rows, to] = jnp.where(first, h0, jnp.where(second, h1, nothing))
                lo_ref[rows, to] = jnp.where(first, l0, jnp.where(second, l1, nothing))

    def prepare(pair):
        mix(2 * pair)
        for b in range(14 * pair, 14 * pair + 14):
            w = stencil(b // 7 + 1, pl.ds(64 * (b % 7), 64))
            high = w.astype(BF16)
            w_hi[64 * b : 64 * b + 64, :] = high
            w_lo[64 * b : 64 * b + 64, :] = (w - high.astype(F32)).astype(BF16)

    for b in range(7):
        rows = pl.ds(64 * b, 64)
        total[rows, :] = stencil(0, rows)
    prepare(0)
    for c in range(DEPTH // CHUNK):
        if c + 1 < TERMS // 2:
            prepare(c + 1)
        at = pl.ds(c * CHUNK, CHUNK)
        dot = lambda x, y: jnp.dot(x[:, at], y[at, :], preferred_element_type=F32)
        total[...] += dot(hi_ref, w_hi) + dot(hi_ref, w_lo) + dot(lo_ref, w_hi)


def flux_kernel(
    faces_ref, field_ref, remote_ref, klq_ref, main_ref, hi_ref, lo_ref, out_ref, steps, coefs, values, total
):
    me = lax.axis_index("mode")
    lane = lane_ids(16)
    limit = faces_ref[0]
    for s in range(1, 4):
        limit = jnp.where(me % 4 == FACE_PLACE[s], faces_ref[s], limit)
    live = (lane < 32) & (32 * (me // 4) + lane < limit)
    coefs[...] = jnp.where(live, 0.5 * (klq_ref[...] + remote_ref[128:144, :]), 0.0)
    first = lane_ids(8) < 32
    for s in range(PARTS):
        packed = face_rows(field_ref, s) - remote_ref[8 * s : 8 * s + 8, :]
        for u in range(7):
            piece = jnp.where(first, lanes(packed, -32 * (u % 4)), 0.0)
            row = HERE * s + 4 * u
            steps[row : row + 4, :] = piece[4 * (u // 4) : 4 * (u // 4) + 4]
    total[...] = coefs[0:1, :] * steps[...]
    for k in range(TERMS):
        w = coefs[k + 1 : k + 2, :] * steps[...]
        high = w.astype(BF16).astype(F32)
        values[MODES * k : MODES * k + MODES, :] = (high + lanes(w - high, 32)).astype(BF16)
    for c in range(DEPTH // CHUNK):
        at = pl.ds(c * CHUNK, CHUNK)
        dot = lambda x: jnp.dot(x[:, at], values[at, :], preferred_element_type=F32)
        total[...] += dot(hi_ref) + dot(lo_ref)
    total[...] = total[...] + lanes(total[...], 96)
    group = lane_ids(4) >> 5
    for s in range(PARTS):
        out_ref[s, 0:HERE, :] = main_ref[HERE * s : HERE * s + HERE, :]
        for v in range(2):
            packed = jnp.zeros((4, 128), F32)
            for u in range(4 * v, min(4 * v + 4, 7)):
                flux = total[HERE * s + 4 * u : HERE * s + 4 * u + 4, :]
                packed = jnp.where(group == u % 4, lanes(flux, 32 * (u % 4)), packed)
            out_ref[s, HERE:32, group_of(v)] = packed


def unpack_kernel(count_ref, tiles_ref, cells_ref, far_out, flux, left_hi, left_lo, added, out_ref, left):
    copies = []
    count = count_ref[0]
    sub = lax.broadcasted_iota(jnp.int32, (8, 128), 0)
    group = lane_ids(8) >> 5
    for s in range(4):
        for tau in range(4):
            value = jnp.zeros((8, 128), F32)
            for q in range(4):
                low = tiles_ref[4 * q + FACE_PLACE[s], 24:32, group_of(tau // 2)]
                even = pltpu.roll(lanes(low, 32 * (q - (2 * tau) % 4)), 4, 0)
                odd = lanes(low, 32 * (q - (2 * tau + 1) % 4))
                value = jnp.where(group == q, jnp.where(sub < 4, even, odd), value)
            if tau == 3:
                value = jnp.where(sub < 4, value, 0.0)
            flux[8 * tau : 8 * tau + 8, group_of(s)] = value
    face_row = [cells_ref[s : s + 1, :] >> 7 for s in range(4)]
    high = [flux[:, group_of(s)].astype(BF16).astype(F32) for s in range(4)]
    low = [flux[:, group_of(s)] - high[s] for s in range(4)]
    for r in range(32):
        for s in range(4):
            at = (pl.ds(32 * r, 32), group_of(s))
            left_hi[at] = jnp.where(face_row[s] == r, high[s], 0.0).astype(BF16)
            left_lo[at] = jnp.where(face_row[s] == r, low[s], 0.0).astype(BF16)
    column = lax.broadcasted_iota(jnp.int32, (128, 128), 0)
    pick = jnp.concatenate(
        [jnp.where((cells_ref[s : s + 1, :] & 127) == column, 1.0, 0.0) for s in range(4)], axis=1
    ).astype(BF16)
    spread = lambda x: lax.dot_general(x[...], pick, (((1,), (1,)), ((), ())), preferred_element_type=F32)
    added[...] = spread(left_hi) + spread(left_lo)
    lane = lane_ids(32)
    group = lane >> 5
    for mr in range(4):
        for v in range(2):
            tiles = [tiles_ref[4 * mr + ml, :, group_of(v)] for ml in range(4)]
            for j in range(4):
                row = 8 * mr + 4 * v + j
                value = lanes(tiles[0], -32 * j)
                for ml in range(1, 4):
                    value = jnp.where(group == ml, lanes(tiles[ml], 32 * (ml - j)), value)
                value = value + added[32 * row : 32 * row + 32, :]
                value = jnp.where(lane + 128 * row < count, value, 0.0)
                out_ref[:, group_of(row)] = value[0:HERE]
        at = pl.ds(1024 * mr, 1024)
        copies.append(pltpu.make_async_copy(out_ref.at[:, at], far_out.at[:, at], left.at[mr]))
        copies[mr].start()
    for copy in copies:
        copy.wait()


def face_route(blocks):
    route = []
    for b in range(blocks):
        for s, offset in enumerate(SLOT_OFFSETS):
            if 0 <= b + offset < blocks:
                for q in range(4):
                    source, target = 4 * q + FACE_PLACE[s], 4 * q + FACE_PLACE[3 - s]
                    route.append((16 * b + source, 16 * (b + offset) + target))
    return route


VMEM = pl.BlockSpec(memory_space=pltpu.VMEM)
SMEM = pl.BlockSpec(memory_space=pltpu.SMEM)
HBM = pl.BlockSpec(memory_space=pl.ANY)


def kernel_call(body, name, shapes, in_specs, scratch, micros, limit, place=None):
    return pl.pallas_call(
        body,
        out_shape=shapes,
        in_specs=in_specs,
        out_specs=tuple(VMEM for _ in shapes) if isinstance(shapes, tuple) else place or VMEM,
        scratch_shapes=scratch,
        compiler_params=pltpu.CompilerParams(vmem_limit_bytes=limit << 20),
        cost_estimate=pl.CostEstimate(flops=int(micros * 1e9), bytes_accessed=int(micros * 1e6), transcendentals=0),
        name=name,
    )


def array(*shape):
    return jax.ShapeDtypeStruct(shape, F32)


def per_device(chaos_field, kl_field, partner, chaos_coef, cell_count, face_count, face_cells):
    cells = face_cells[0]
    far = lambda each: pltpu.with_memory_space_constraint(each, pltpu.HBM)
    send, coefs, klq = kernel_call(
        pack_kernel,
        "pack",
        (array(PARTS, 32, 384), array(4, 16, 256), array(16, 128)),
        [SMEM, HBM, HBM, HBM, HBM, HBM],
        [
            pltpu.VMEM(cells.shape, jnp.int32),
            pltpu.VMEM((HERE, 4096), F32),
            pltpu.VMEM(kl_field.shape, F32),
            pltpu.VMEM((16, 4096), F32),
            pltpu.VMEM((PARTS, 16, 384), F32),
            pltpu.VMEM(partner.shape, jnp.int32),
            pltpu.VMEM(chaos_coef.shape, F32),
            pltpu.VMEM((128, 128), F32),
            pltpu.SemaphoreType.DMA((8,)),
        ],
        4,
        8,
    )(cell_count, far(chaos_field), far(kl_field), far(cells), far(partner), far(chaos_coef))
    field = lax.all_to_all(send, "mode", 0, 0, tiled=True)
    outgoing = kernel_call(outgoing_kernel, "outgoing", array(144, 128), [VMEM] * 2, [], 0.5, 4)(field, klq)
    remote = lax.ppermute(outgoing, ("blk", "mode"), face_route(lax.axis_size("blk")))
    mix = jax.ShapeDtypeStruct((MODES, DEPTH), BF16)
    main, mix_hi, mix_lo = kernel_call(
        apply_kernel,
        "apply",
        (array(MODES, 256), mix, mix),
        [VMEM] * 2,
        [
            pltpu.VMEM((4, MODES, 256), F32),
            pltpu.VMEM((MODES, 128), F32),
            pltpu.VMEM((DEPTH, 256), BF16),
            pltpu.VMEM((DEPTH, 256), BF16),
        ],
        8,
        24,
    )(field, coefs)
    tiles = kernel_call(
        flux_kernel,
        "flux",
        array(PARTS, 32, 256),
        [SMEM] + [VMEM] * 6,
        [
            pltpu.VMEM((MODES, 128), F32),
            pltpu.VMEM((16, 128), F32),
            pltpu.VMEM((DEPTH, 128), BF16),
            pltpu.VMEM((MODES, 128), F32),
        ],
        4,
        8,
    )(face_count[0], field, remote, klq, main, mix_hi, mix_lo)
    back = lax.all_to_all(tiles, "mode", 0, 0, tiled=True)
    return kernel_call(
        unpack_kernel,
        "unpack",
        jax.ShapeDtypeStruct(chaos_field.shape, F32),
        [SMEM, VMEM, VMEM],
        [
            pltpu.VMEM((32, 512), F32),
            pltpu.VMEM((1024, 512), BF16),
            pltpu.VMEM((1024, 512), BF16),
            pltpu.VMEM((1024, 128), F32),
            pltpu.VMEM((HERE, 4096), F32),
            pltpu.SemaphoreType.DMA((4,)),
        ],
        3,
        8,
        HBM,
    )(cell_count, back, cells)


def solution(mesh):
    in_specs = (
        P("mode", "blk"),
        P(None, "blk"),
        P(None, None, "mode"),
        P(None, None, "mode"),
        P("blk"),
        P("blk", None),
        P("blk", None, None),
    )
    return jax.shard_map(
        per_device, mesh=mesh, in_specs=in_specs, out_specs=P("mode", "blk"), check_vma=False
    )
```

```python
import jax
import jax.numpy as jnp
from jax import lax
from jax.experimental import pallas as pl
from jax.experimental.pallas import tpu as pltpu
from jax.sharding import PartitionSpec as P

SLOT_OFFSETS = (-2, -1, 1, 2)
FACE_PLACE = (0, 2, 3, 1)
F32 = jnp.float32
BF16 = jnp.bfloat16
TERMS = 12
MODES = 448
PARTS = 16
HERE = MODES // PARTS
DEPTH = TERMS * MODES
CHUNK = 768


def lanes(value, shift):
    shift = shift % 128
    return value if shift == 0 else pltpu.roll(value, shift, 1)


def lane_ids(rows):
    return lax.broadcasted_iota(jnp.int32, (rows, 128), 1)


def along(value, index):
    return jnp.take_along_axis(value, index, axis=1, mode="promise_in_bounds")


def group_of(v):
    return pl.ds(128 * v, 128)


def pack_rows(load, rows, mr, out_ref):
    group = lane_ids(rows) >> 5
    for v in range(2):
        cells = [load(8 * mr + 4 * v + j) for j in range(4)]
        for ml in range(4):
            tile = lanes(cells[0], -32 * ml)
            for j in range(1, 4):
                tile = jnp.where(group == j, lanes(cells[j], 32 * (j - ml)), tile)
            out_ref[4 * mr + ml, 0:rows, group_of(v)] = tile


def pack_halo(rows, m, out_ref, table):
    lane = lane_ids(rows)
    left_pick = jnp.where((lane >= 64) & (lane < 72), 32 * (lane & 3) + 31, 0)
    right_pick = jnp.where((lane >= 72) & (lane < 80), 32 * (lane & 3), 0)
    halo = table
    if m >= 4:
        halo = jnp.where(lane < 32, lanes(out_ref[m - 4, 0:rows, group_of(1)], 32), halo)
    if m < 12:
        below = lanes(out_ref[m + 4, 0:rows, group_of(0)], 32)
        halo = jnp.where((lane >= 32) & (lane < 64), below, halo)
    for v in range(2):
        if m % 4 > 0:
            side = along(out_ref[m - 1, 0:rows, group_of(v)], left_pick)
            halo = jnp.where((lane >= 64 + 4 * v) & (lane < 68 + 4 * v), side, halo)
        if m % 4 < 3:
            side = along(out_ref[m + 1, 0:rows, group_of(v)], right_pick)
            halo = jnp.where((lane >= 72 + 4 * v) & (lane < 76 + 4 * v), side, halo)
    out_ref[m, 0:rows, group_of(2)] = halo


def pack_kernel(
    count_ref, far_field, far_kl, far_cells, far_partner, far_coef, send_ref, coefs_ref, klq_ref,
    cells_ref, field_ref, kl_ref, kl_pad, partner_ref, coef_ref, stage, arrived,
):
    copies = [
        pltpu.make_async_copy(far_partner, partner_ref, arrived.at[4]),
        pltpu.make_async_copy(far_coef, coef_ref, arrived.at[5]),
        pltpu.make_async_copy(far_cells, cells_ref, arrived.at[7]),
        pltpu.make_async_copy(far_kl, kl_ref, arrived.at[6]),
    ]
    blocks = [
        pltpu.make_async_copy(far_field.at[:, pl.ds(1024 * i, 1024)], field_ref.at[:, pl.ds(1024 * i, 1024)], arrived.at[i])
        for i in range(4)
    ]
    for copy in copies + blocks:
        copy.start()
    stage[...] = jnp.zeros((128, 128), F32)
    for copy in copies:
        copy.wait()
    for k in range(TERMS):
        mode, coef = partner_ref[k], coef_ref[k]
        same = mode[0:1] == mode[1:2]
        stage[80 + k : 81 + k, 0:HERE] = mode[0:1].astype(F32)
        stage[92 + k : 93 + k, 0:HERE] = mode[1:2].astype(F32)
        stage[104 + k : 105 + k, 0:HERE] = coef[0:1] + jnp.where(same, coef[1:2], 0.0)
        stage[116 + k : 117 + k, 0:HERE] = coef[1:2]
    table = stage[...].T[0:HERE]
    kl_pad[0:13, :] = kl_ref[...]
    kl_pad[13:16, :] = jnp.zeros((3, 4096), F32)
    face_coefficients(count_ref, cells_ref, coefs_ref, klq_ref, kl_pad)
    count = count_ref[0]
    lane = lane_ids(HERE)
    cells = cells_ref[...]
    faces = [jnp.zeros((HERE, 128), F32) for _ in range(4)]
    picks = [jnp.broadcast_to(cells[s : s + 1] & 127, (HERE, 128)) for s in range(4)]
    live = lambda r: jnp.where(lane + 128 * r < count, field_ref[:, group_of(r)], 0.0)
    for mr in range(4):
        blocks[mr].wait()
        for r in range(8 * mr, 8 * mr + 8):
            row = live(r)
            for s in range(4):
                faces[s] = jnp.where(cells[s : s + 1] >> 7 == r, along(row, picks[s]), faces[s])
        pack_rows(live, HERE, mr, send_ref)
    group = lane_ids(4) >> 5
    for s in range(4):
        turned = [lanes(faces[s], 32 * t) for t in range(4)]
        for q in range(4):
            m = 4 * q + FACE_PLACE[s]
            for v in range(2):
                packed = jnp.zeros((4, 128), F32)
                for u in range(4 * v, min(4 * v + 4, 7)):
                    packed = jnp.where(group == u % 4, turned[(u - q) % 4][4 * u : 4 * u + 4], packed)
                send_ref[m, HERE:32, group_of(v)] = packed
            send_ref[m, HERE:32, group_of(2)] = jnp.zeros((4, 128), F32)
    copies = []
    for m in range(PARTS):
        pack_halo(HERE, m, send_ref, table)


def neighbours(first, second, halo):
    rows = first.shape[0]
    lane = lane_ids(rows)
    up_first, up_second = lanes(first, 32), lanes(second, 32)
    down_first, down_second = lanes(first, -32), lanes(second, -32)
    up = (jnp.where(lane < 32, halo, up_first), jnp.where(lane < 32, up_first, up_second))
    down = (jnp.where(lane < 96, down_first, down_second), jnp.where(lane < 96, down_second, lanes(halo, 64)))
    column = lane & 31
    left, right = [], []
    for v, cells in enumerate((first, second)):
        left_halo = along(halo, 64 + 4 * v + (lane >> 5))
        right_halo = along(halo, 72 + 4 * v + (lane >> 5))
        left.append(jnp.where(column == 0, left_halo, lanes(cells, 1)))
        right.append(jnp.where(column == 31, right_halo, lanes(cells, -1)))
    return up, down, left, right


def face_coefficients(count_ref, cells_ref, coefs_ref, klq_ref, source):
    me = lax.axis_index("mode")
    mr, ml = me // 4, me % 4
    count = count_ref[0]
    lane = lane_ids(16)
    group = lane >> 5
    load = lambda r: source[:, pl.ds(pl.multiple_of(128 * r, 128), 128)]
    turn = lambda value, steps: pltpu.roll(value, 32 * (steps & 3), 1)
    rows = [load(8 * mr + r) for r in range(8)]
    a = []
    for v in range(2):
        tile = turn(rows[4 * v], -ml)
        for j in range(1, 4):
            tile = jnp.where(group == j, turn(rows[4 * v + j], j - ml), tile)
        a.append(tile)
    halo = turn(load(jnp.maximum(8 * mr - 1, 0)), -ml)
    halo = jnp.where(group == 1, turn(load(jnp.minimum(8 * mr + 8, 31)), 1 - ml), halo)
    before = jnp.full((16, 128), jnp.maximum(32 * ml - 1, 0), jnp.int32)
    after = jnp.full((16, 128), jnp.minimum(32 * ml + 32, 127), jnp.int32)
    for r in range(8):
        halo = jnp.where(lane == 64 + r, along(rows[r], before), halo)
        halo = jnp.where(lane == 72 + r, along(rows[r], after), halo)
    a.append(halo)
    cell = cells_ref[0:1]
    for s in range(1, 4):
        cell = jnp.where(ml == FACE_PLACE[s], cells_ref[s : s + 1], cell)
    pick = jnp.broadcast_to(cell & 127, (16, 128))
    own = jnp.zeros((16, 128), F32)
    for r in range(32):
        own = jnp.where(cell >> 7 == r, along(source[:, group_of(r)], pick), own)
    klq_ref[...] = turn(own, -mr)
    around = neighbours(*a)
    for v in range(2):
        row = 8 * mr + 4 * v + (lane >> 5)
        column = 32 * ml + (lane & 31)
        cell = 128 * row + column
        here = cell < count
        there = (
            (row > 0) & (cell - 128 < count),
            (row < 31) & (cell + 128 < count),
            (column > 0) & (cell - 1 < count),
            (column < 127) & (cell + 1 < count),
        )
        for d in range(4):
            value = 0.5 * (a[v] + around[d][v])
            coefs_ref[d, :, group_of(v)] = jnp.where(here & there[d], value, 0.0)


def face_rows(field_ref, s):
    low = field_ref[s, 24:32, group_of(0)]
    sub = lax.broadcasted_iota(jnp.int32, (8, 128), 0)
    return jnp.where(sub < 4, pltpu.roll(low, 4, 0), field_ref[s, 24:32, group_of(1)])


def outgoing_kernel(field_ref, klq_ref, out_ref):
    for s in range(PARTS):
        out_ref[8 * s : 8 * s + 8, :] = face_rows(field_ref, s)
    out_ref[128:144, :] = klq_ref[...]


def apply_kernel(field_ref, coefs_ref, total, hi_ref, lo_ref, steps, table, w_hi, w_lo):
    for s in range(PARTS):
        rows = pl.ds(HERE * s, HERE)
        cells = [field_ref[s, 0:HERE, group_of(v)] for v in range(3)]
        around = neighbours(*cells)
        for d in range(4):
            for v in range(2):
                steps[d, rows, group_of(v)] = cells[v] - around[d][v]
        table[rows, :] = cells[2]

    def stencil(k, rows):
        w = coefs_ref[0, k : k + 1, :] * steps[0, rows, :]
        for d in range(1, 4):
            w = w + coefs_ref[d, k : k + 1, :] * steps[d, rows, :]
        return w

    lane = lax.broadcasted_iota(jnp.int16, (16, 128), 1)
    nothing = jnp.zeros((16, 128), BF16)

    def mix(k):
        for c in range(MODES // 16):
            rows = pl.ds(16 * c, 16)
            entry = table[rows, :]
            wide = []
            for kk in (k, k + 1):
                cols = [entry[:, 80 + 12 * t + kk : 81 + 12 * t + kk] for t in range(4)]
                high = [col.astype(BF16) for col in cols[2:]]
                low = [(col - h.astype(F32)).astype(BF16) for col, h in zip(cols[2:], high)]
                modes = [col.astype(jnp.int32).astype(jnp.int16) for col in cols[:2]]
                wide.append([jnp.broadcast_to(part, (16, 128)) for part in modes + high + low])
            for g in range(7):
                if g < 3:
                    first, second, h0, h1, l0, l1 = wide[0]
                    at = lane + jnp.int16(128 * g)
                elif g == 3:
                    first, second, h0, h1, l0, l1 = (jnp.where(lane < 64, a, b) for a, b in zip(*wide))
                    at = jnp.where(lane < 64, lane + jnp.int16(384), lane - jnp.int16(64))
                else:
                    first, second, h0, h1, l0, l1 = wide[1]
                    at = lane + jnp.int16(128 * g - MODES)
                first, second = first == at, second == at
                to = pl.ds(MODES * k + 128 * g, 128)
                hi_ref[rows, to] = jnp.where(first, h0, jnp.where(second, h1, nothing))
                lo_ref[rows, to] = jnp.where(first, l0, jnp.where(second, l1, nothing))

    def prepare(pair):
        mix(2 * pair)
        for b in range(14 * pair, 14 * pair + 14):
            w = stencil(b // 7 + 1, pl.ds(64 * (b % 7), 64))
            high = w.astype(BF16)
            w_hi[64 * b : 64 * b + 64, :] = high
            w_lo[64 * b : 64 * b + 64, :] = (w - high.astype(F32)).astype(BF16)

    for b in range(7):
        rows = pl.ds(64 * b, 64)
        total[rows, :] = stencil(0, rows)
    prepare(0)
    for c in range(DEPTH // CHUNK):
        if c + 1 < TERMS // 2:
            prepare(c + 1)
        at = pl.ds(c * CHUNK, CHUNK)
        dot = lambda x, y: jnp.dot(x[:, at], y[at, :], preferred_element_type=F32)
        total[...] += dot(hi_ref, w_hi) + dot(hi_ref, w_lo) + dot(lo_ref, w_hi)


def flux_kernel(
    faces_ref, field_ref, remote_ref, klq_ref, main_ref, hi_ref, lo_ref, out_ref, steps, coefs, values, total
):
    me = lax.axis_index("mode")
    lane = lane_ids(16)
    limit = faces_ref[0]
    for s in range(1, 4):
        limit = jnp.where(me % 4 == FACE_PLACE[s], faces_ref[s], limit)
    live = (lane < 32) & (32 * (me // 4) + lane < limit)
    coefs[...] = jnp.where(live, 0.5 * (klq_ref[...] + remote_ref[128:144, :]), 0.0)
    first = lane_ids(8) < 32
    for s in range(PARTS):
        packed = face_rows(field_ref, s) - remote_ref[8 * s : 8 * s + 8, :]
        for u in range(7):
            piece = jnp.where(first, lanes(packed, -32 * (u % 4)), 0.0)
            row = HERE * s + 4 * u
            steps[row : row + 4, :] = piece[4 * (u // 4) : 4 * (u // 4) + 4]
    total[...] = coefs[0:1, :] * steps[...]
    for k in range(TERMS):
        w = coefs[k + 1 : k + 2, :] * steps[...]
        high = w.astype(BF16).astype(F32)
        values[MODES * k : MODES * k + MODES, :] = (high + lanes(w - high, 32)).astype(BF16)
    for c in range(DEPTH // CHUNK):
        at = pl.ds(c * CHUNK, CHUNK)
        dot = lambda x: jnp.dot(x[:, at], values[at, :], preferred_element_type=F32)
        total[...] += dot(hi_ref) + dot(lo_ref)
    total[...] = total[...] + lanes(total[...], 96)
    group = lane_ids(4) >> 5
    for s in range(PARTS):
        out_ref[s, 0:HERE, :] = main_ref[HERE * s : HERE * s + HERE, :]
        for v in range(2):
            packed = jnp.zeros((4, 128), F32)
            for u in range(4 * v, min(4 * v + 4, 7)):
                flux = total[HERE * s + 4 * u : HERE * s + 4 * u + 4, :]
                packed = jnp.where(group == u % 4, lanes(flux, 32 * (u % 4)), packed)
            out_ref[s, HERE:32, group_of(v)] = packed


def unpack_kernel(count_ref, tiles_ref, cells_ref, far_out, flux, left_hi, left_lo, added, out_ref, left):
    copies = []
    count = count_ref[0]
    sub = lax.broadcasted_iota(jnp.int32, (8, 128), 0)
    group = lane_ids(8) >> 5
    for s in range(4):
        for tau in range(4):
            value = jnp.zeros((8, 128), F32)
            for q in range(4):
                low = tiles_ref[4 * q + FACE_PLACE[s], 24:32, group_of(tau // 2)]
                even = pltpu.roll(lanes(low, 32 * (q - (2 * tau) % 4)), 4, 0)
                odd = lanes(low, 32 * (q - (2 * tau + 1) % 4))
                value = jnp.where(group == q, jnp.where(sub < 4, even, odd), value)
            if tau == 3:
                value = jnp.where(sub < 4, value, 0.0)
            flux[8 * tau : 8 * tau + 8, group_of(s)] = value
    face_row = [cells_ref[s : s + 1, :] >> 7 for s in range(4)]
    high = [flux[:, group_of(s)].astype(BF16).astype(F32) for s in range(4)]
    low = [flux[:, group_of(s)] - high[s] for s in range(4)]
    for r in range(32):
        for s in range(4):
            at = (pl.ds(32 * r, 32), group_of(s))
            left_hi[at] = jnp.where(face_row[s] == r, high[s], 0.0).astype(BF16)
            left_lo[at] = jnp.where(face_row[s] == r, low[s], 0.0).astype(BF16)
    column = lax.broadcasted_iota(jnp.int32, (128, 128), 0)
    pick = jnp.concatenate(
        [jnp.where((cells_ref[s : s + 1, :] & 127) == column, 1.0, 0.0) for s in range(4)], axis=1
    ).astype(BF16)
    spread = lambda x: lax.dot_general(x[...], pick, (((1,), (1,)), ((), ())), preferred_element_type=F32)
    added[...] = spread(left_hi) + spread(left_lo)
    lane = lane_ids(32)
    group = lane >> 5
    for mr in range(4):
        for v in range(2):
            tiles = [tiles_ref[4 * mr + ml, :, group_of(v)] for ml in range(4)]
            for j in range(4):
                row = 8 * mr + 4 * v + j
                value = lanes(tiles[0], -32 * j)
                for ml in range(1, 4):
                    value = jnp.where(group == ml, lanes(tiles[ml], 32 * (ml - j)), value)
                value = value + added[32 * row : 32 * row + 32, :]
                value = jnp.where(lane + 128 * row < count, value, 0.0)
                out_ref[:, group_of(row)] = value[0:HERE]
        at = pl.ds(1024 * mr, 1024)
        copies.append(pltpu.make_async_copy(out_ref.at[:, at], far_out.at[:, at], left.at[mr]))
        copies[mr].start()
    for copy in copies:
        copy.wait()


def face_route(blocks):
    route = []
    for b in range(blocks):
        for s, offset in enumerate(SLOT_OFFSETS):
            if 0 <= b + offset < blocks:
                for q in range(4):
                    source, target = 4 * q + FACE_PLACE[s], 4 * q + FACE_PLACE[3 - s]
                    route.append((16 * b + source, 16 * (b + offset) + target))
    return route


VMEM = pl.BlockSpec(memory_space=pltpu.VMEM)
SMEM = pl.BlockSpec(memory_space=pltpu.SMEM)
HBM = pl.BlockSpec(memory_space=pl.ANY)


def kernel_call(body, name, shapes, in_specs, scratch, micros, limit, place=None):
    return pl.pallas_call(
        body,
        out_shape=shapes,
        in_specs=in_specs,
        out_specs=tuple(VMEM for _ in shapes) if isinstance(shapes, tuple) else place or VMEM,
        scratch_shapes=scratch,
        compiler_params=pltpu.CompilerParams(vmem_limit_bytes=limit << 20),
        cost_estimate=pl.CostEstimate(flops=int(micros * 1e9), bytes_accessed=int(micros * 1e6), transcendentals=0),
        name=name,
    )


def array(*shape):
    return jax.ShapeDtypeStruct(shape, F32)


def per_device(chaos_field, kl_field, partner, chaos_coef, cell_count, face_count, face_cells):
    cells = face_cells[0]
    far = lambda each: pltpu.with_memory_space_constraint(each, pltpu.HBM)
    send, coefs, klq = kernel_call(
        pack_kernel,
        "pack",
        (array(PARTS, 32, 384), array(4, 16, 256), array(16, 128)),
        [SMEM, HBM, HBM, HBM, HBM, HBM],
        [
            pltpu.VMEM(cells.shape, jnp.int32),
            pltpu.VMEM((HERE, 4096), F32),
            pltpu.VMEM(kl_field.shape, F32),
            pltpu.VMEM((16, 4096), F32),
            pltpu.VMEM(partner.shape, jnp.int32),
            pltpu.VMEM(chaos_coef.shape, F32),
            pltpu.VMEM((128, 128), F32),
            pltpu.SemaphoreType.DMA((8,)),
        ],
        4,
        8,
    )(cell_count, far(chaos_field), far(kl_field), far(cells), far(partner), far(chaos_coef))
    field = lax.all_to_all(send, "mode", 0, 0, tiled=True)
    outgoing = kernel_call(outgoing_kernel, "outgoing", array(144, 128), [VMEM] * 2, [], 0.5, 4)(field, klq)
    remote = lax.ppermute(outgoing, ("blk", "mode"), face_route(lax.axis_size("blk")))
    mix = jax.ShapeDtypeStruct((MODES, DEPTH), BF16)
    main, mix_hi, mix_lo = kernel_call(
        apply_kernel,
        "apply",
        (array(MODES, 256), mix, mix),
        [VMEM] * 2,
        [
            pltpu.VMEM((4, MODES, 256), F32),
            pltpu.VMEM((MODES, 128), F32),
            pltpu.VMEM((DEPTH, 256), BF16),
            pltpu.VMEM((DEPTH, 256), BF16),
        ],
        8,
        24,
    )(field, coefs)
    tiles = kernel_call(
        flux_kernel,
        "flux",
        array(PARTS, 32, 256),
        [SMEM] + [VMEM] * 6,
        [
            pltpu.VMEM((MODES, 128), F32),
            pltpu.VMEM((16, 128), F32),
            pltpu.VMEM((DEPTH, 128), BF16),
            pltpu.VMEM((MODES, 128), F32),
        ],
        4,
        8,
    )(face_count[0], field, remote, klq, main, mix_hi, mix_lo)
    back = lax.all_to_all(tiles, "mode", 0, 0, tiled=True)
    return kernel_call(
        unpack_kernel,
        "unpack",
        jax.ShapeDtypeStruct(chaos_field.shape, F32),
        [SMEM, VMEM, VMEM],
        [
            pltpu.VMEM((32, 512), F32),
            pltpu.VMEM((1024, 512), BF16),
            pltpu.VMEM((1024, 512), BF16),
            pltpu.VMEM((1024, 128), F32),
            pltpu.VMEM((HERE, 4096), F32),
            pltpu.SemaphoreType.DMA((4,)),
        ],
        3,
        8,
        HBM,
    )(cell_count, back, cells)


def solution(mesh):
    in_specs = (
        P("mode", "blk"),
        P(None, "blk"),
        P(None, None, "mode"),
        P(None, None, "mode"),
        P("blk"),
        P("blk", None),
        P("blk", None, None),
    )
    return jax.shard_map(
        per_device, mesh=mesh, in_specs=in_specs, out_specs=P("mode", "blk"), check_vma=False
    )
```

```python
import jax
import jax.numpy as jnp
from jax import lax
from jax.experimental import pallas as pl
from jax.experimental.pallas import tpu as pltpu
from jax.sharding import PartitionSpec as P

SLOT_OFFSETS = (-2, -1, 1, 2)
FACE_PLACE = (0, 2, 3, 1)
F32 = jnp.float32
BF16 = jnp.bfloat16
TERMS = 12
MODES = 448
PARTS = 16
HERE = MODES // PARTS
DEPTH = TERMS * MODES
CHUNK = 768


def lanes(value, shift):
    shift = shift % 128
    return value if shift == 0 else pltpu.roll(value, shift, 1)


def lane_ids(rows):
    return lax.broadcasted_iota(jnp.int32, (rows, 128), 1)


def along(value, index):
    return jnp.take_along_axis(value, index, axis=1, mode="promise_in_bounds")


def group_of(v):
    return pl.ds(128 * v, 128)


def pack_rows(load, rows, mr, out_ref):
    group = lane_ids(rows) >> 5
    for v in range(2):
        cells = [load(8 * mr + 4 * v + j) for j in range(4)]
        for ml in range(4):
            tile = lanes(cells[0], -32 * ml)
            for j in range(1, 4):
                tile = jnp.where(group == j, lanes(cells[j], 32 * (j - ml)), tile)
            out_ref[4 * mr + ml, 0:rows, group_of(v)] = tile


def pack_halo(rows, m, out_ref, table):
    lane = lane_ids(rows)
    left_pick = jnp.where((lane >= 64) & (lane < 72), 32 * (lane & 3) + 31, 0)
    right_pick = jnp.where((lane >= 72) & (lane < 80), 32 * (lane & 3), 0)
    halo = table
    if m >= 4:
        halo = jnp.where(lane < 32, lanes(out_ref[m - 4, 0:rows, group_of(1)], 32), halo)
    if m < 12:
        below = lanes(out_ref[m + 4, 0:rows, group_of(0)], 32)
        halo = jnp.where((lane >= 32) & (lane < 64), below, halo)
    for v in range(2):
        if m % 4 > 0:
            side = along(out_ref[m - 1, 0:rows, group_of(v)], left_pick)
            halo = jnp.where((lane >= 64 + 4 * v) & (lane < 68 + 4 * v), side, halo)
        if m % 4 < 3:
            side = along(out_ref[m + 1, 0:rows, group_of(v)], right_pick)
            halo = jnp.where((lane >= 72 + 4 * v) & (lane < 76 + 4 * v), side, halo)
    out_ref[m, 0:rows, group_of(2)] = halo


def pack_kernel(
    count_ref, far_field, far_kl, far_cells, far_partner, far_coef, send_ref, coefs_ref, klq_ref,
    cells_ref, field_ref, kl_ref, kl_pad, partner_ref, coef_ref, stage, arrived,
):
    copies = [
        pltpu.make_async_copy(far_partner, partner_ref, arrived.at[4]),
        pltpu.make_async_copy(far_coef, coef_ref, arrived.at[5]),
        pltpu.make_async_copy(far_cells, cells_ref, arrived.at[7]),
        pltpu.make_async_copy(far_kl, kl_ref, arrived.at[6]),
    ]
    blocks = [
        pltpu.make_async_copy(far_field.at[:, pl.ds(1024 * i, 1024)], field_ref.at[:, pl.ds(1024 * i, 1024)], arrived.at[i])
        for i in range(4)
    ]
    for copy in copies + blocks:
        copy.start()
    stage[...] = jnp.zeros((128, 128), F32)
    for copy in copies:
        copy.wait()
    for k in range(TERMS):
        mode, coef = partner_ref[k], coef_ref[k]
        same = mode[0:1] == mode[1:2]
        stage[80 + k : 81 + k, 0:HERE] = mode[0:1].astype(F32)
        stage[92 + k : 93 + k, 0:HERE] = mode[1:2].astype(F32)
        stage[104 + k : 105 + k, 0:HERE] = coef[0:1] + jnp.where(same, coef[1:2], 0.0)
        stage[116 + k : 117 + k, 0:HERE] = coef[1:2]
    table = stage[...].T[0:HERE]
    kl_pad[0:13, :] = kl_ref[...]
    kl_pad[13:16, :] = jnp.zeros((3, 4096), F32)
    face_coefficients(count_ref, cells_ref, coefs_ref, klq_ref, kl_pad)
    count = count_ref[0]
    lane = lane_ids(HERE)
    cells = cells_ref[...]
    faces = [jnp.zeros((HERE, 128), F32) for _ in range(4)]
    picks = [jnp.broadcast_to(cells[s : s + 1] & 127, (HERE, 128)) for s in range(4)]
    live = lambda r: jnp.where(lane + 128 * r < count, field_ref[:, group_of(r)], 0.0)
    for mr in range(4):
        blocks[mr].wait()
        for r in range(8 * mr, 8 * mr + 8):
            row = live(r)
            for s in range(4):
                faces[s] = jnp.where(cells[s : s + 1] >> 7 == r, along(row, picks[s]), faces[s])
        pack_rows(live, HERE, mr, send_ref)
    group = lane_ids(4) >> 5
    for s in range(4):
        turned = [lanes(faces[s], 32 * t) for t in range(4)]
        for q in range(4):
            m = 4 * q + FACE_PLACE[s]
            for v in range(2):
                packed = jnp.zeros((4, 128), F32)
                for u in range(4 * v, min(4 * v + 4, 7)):
                    packed = jnp.where(group == u % 4, turned[(u - q) % 4][4 * u : 4 * u + 4], packed)
                send_ref[m, HERE:32, group_of(v)] = packed
            send_ref[m, HERE:32, group_of(2)] = jnp.zeros((4, 128), F32)
    copies = []
    for m in range(PARTS):
        pack_halo(HERE, m, send_ref, table)


def neighbours(first, second, halo):
    rows = first.shape[0]
    lane = lane_ids(rows)
    up_first, up_second = lanes(first, 32), lanes(second, 32)
    down_first, down_second = lanes(first, -32), lanes(second, -32)
    up = (jnp.where(lane < 32, halo, up_first), jnp.where(lane < 32, up_first, up_second))
    down = (jnp.where(lane < 96, down_first, down_second), jnp.where(lane < 96, down_second, lanes(halo, 64)))
    column = lane & 31
    left, right = [], []
    for v, cells in enumerate((first, second)):
        left_halo = along(halo, 64 + 4 * v + (lane >> 5))
        right_halo = along(halo, 72 + 4 * v + (lane >> 5))
        left.append(jnp.where(column == 0, left_halo, lanes(cells, 1)))
        right.append(jnp.where(column == 31, right_halo, lanes(cells, -1)))
    return up, down, left, right


def face_coefficients(count_ref, cells_ref, coefs_ref, klq_ref, source):
    me = lax.axis_index("mode")
    mr, ml = me // 4, me % 4
    count = count_ref[0]
    lane = lane_ids(16)
    group = lane >> 5
    load = lambda r: source[:, pl.ds(pl.multiple_of(128 * r, 128), 128)]
    turn = lambda value, steps: pltpu.roll(value, 32 * (steps & 3), 1)
    rows = [load(8 * mr + r) for r in range(8)]
    a = []
    for v in range(2):
        tile = turn(rows[4 * v], -ml)
        for j in range(1, 4):
            tile = jnp.where(group == j, turn(rows[4 * v + j], j - ml), tile)
        a.append(tile)
    halo = turn(load(jnp.maximum(8 * mr - 1, 0)), -ml)
    halo = jnp.where(group == 1, turn(load(jnp.minimum(8 * mr + 8, 31)), 1 - ml), halo)
    before = jnp.full((16, 128), jnp.maximum(32 * ml - 1, 0), jnp.int32)
    after = jnp.full((16, 128), jnp.minimum(32 * ml + 32, 127), jnp.int32)
    for r in range(8):
        halo = jnp.where(lane == 64 + r, along(rows[r], before), halo)
        halo = jnp.where(lane == 72 + r, along(rows[r], after), halo)
    a.append(halo)
    cell = cells_ref[0:1]
    for s in range(1, 4):
        cell = jnp.where(ml == FACE_PLACE[s], cells_ref[s : s + 1], cell)
    pick = jnp.broadcast_to(cell & 127, (16, 128))
    own = jnp.zeros((16, 128), F32)
    for r in range(32):
        own = jnp.where(cell >> 7 == r, along(source[:, group_of(r)], pick), own)
    klq_ref[...] = turn(own, -mr)
    around = neighbours(*a)
    for v in range(2):
        row = 8 * mr + 4 * v + (lane >> 5)
        column = 32 * ml + (lane & 31)
        cell = 128 * row + column
        here = cell < count
        there = (
            (row > 0) & (cell - 128 < count),
            (row < 31) & (cell + 128 < count),
            (column > 0) & (cell - 1 < count),
            (column < 127) & (cell + 1 < count),
        )
        for d in range(4):
            value = 0.5 * (a[v] + around[d][v])
            coefs_ref[d, :, group_of(v)] = jnp.where(here & there[d], value, 0.0)


def face_rows(field_ref, s):
    low = field_ref[s, 24:32, group_of(0)]
    sub = lax.broadcasted_iota(jnp.int32, (8, 128), 0)
    return jnp.where(sub < 4, pltpu.roll(low, 4, 0), field_ref[s, 24:32, group_of(1)])


def outgoing_kernel(field_ref, klq_ref, out_ref):
    for s in range(PARTS):
        out_ref[8 * s : 8 * s + 8, :] = face_rows(field_ref, s)
    out_ref[128:144, :] = klq_ref[...]


def apply_kernel(field_ref, coefs_ref, total, hi_ref, lo_ref, steps, inside, w_hi, w_lo):
    for s in range(PARTS):
        inside[HERE * s : HERE * s + HERE, :] = field_ref[s, 0:HERE, :]
    for b in range(MODES // 32):
        rows = pl.ds(32 * b, 32)
        cells = [inside[rows, group_of(v)] for v in range(3)]
        around = neighbours(*cells)
        for d in range(4):
            for v in range(2):
                steps[d, rows, group_of(v)] = cells[v] - around[d][v]

    def stencil(k, rows):
        w = coefs_ref[0, k : k + 1, :] * steps[0, rows, :]
        for d in range(1, 4):
            w = w + coefs_ref[d, k : k + 1, :] * steps[d, rows, :]
        return w

    lane = lax.broadcasted_iota(jnp.int16, (16, 128), 1)
    nothing = jnp.zeros((16, 128), BF16)

    def mix(k):
        for c in range(MODES // 16):
            rows = pl.ds(16 * c, 16)
            entry = inside[rows, group_of(2)]
            wide = []
            for kk in (k, k + 1):
                cols = [entry[:, 80 + 12 * t + kk : 81 + 12 * t + kk] for t in range(4)]
                high = [col.astype(BF16) for col in cols[2:]]
                low = [(col - h.astype(F32)).astype(BF16) for col, h in zip(cols[2:], high)]
                modes = [col.astype(jnp.int32).astype(jnp.int16) for col in cols[:2]]
                wide.append([jnp.broadcast_to(part, (16, 128)) for part in modes + high + low])
            for g in range(7):
                if g < 3:
                    first, second, h0, h1, l0, l1 = wide[0]
                    at = lane + jnp.int16(128 * g)
                elif g == 3:
                    first, second, h0, h1, l0, l1 = (jnp.where(lane < 64, a, b) for a, b in zip(*wide))
                    at = jnp.where(lane < 64, lane + jnp.int16(384), lane - jnp.int16(64))
                else:
                    first, second, h0, h1, l0, l1 = wide[1]
                    at = lane + jnp.int16(128 * g - MODES)
                first, second = first == at, second == at
                to = pl.ds(MODES * k + 128 * g, 128)
                hi_ref[rows, to] = jnp.where(first, h0, jnp.where(second, h1, nothing))
                lo_ref[rows, to] = jnp.where(first, l0, jnp.where(second, l1, nothing))

    def prepare(pair):
        mix(2 * pair)
        for b in range(14 * pair, 14 * pair + 14):
            w = stencil(b // 7 + 1, pl.ds(64 * (b % 7), 64))
            high = w.astype(BF16)
            w_hi[64 * b : 64 * b + 64, :] = high
            w_lo[64 * b : 64 * b + 64, :] = (w - high.astype(F32)).astype(BF16)

    for b in range(7):
        rows = pl.ds(64 * b, 64)
        total[rows, :] = stencil(0, rows)
    prepare(0)
    for c in range(DEPTH // CHUNK):
        if c + 1 < TERMS // 2:
            prepare(c + 1)
        at = pl.ds(c * CHUNK, CHUNK)
        dot = lambda x, y: jnp.dot(x[:, at], y[at, :], preferred_element_type=F32)
        total[...] += dot(hi_ref, w_hi) + dot(hi_ref, w_lo) + dot(lo_ref, w_hi)


def flux_kernel(
    faces_ref, field_ref, remote_ref, klq_ref, main_ref, hi_ref, lo_ref, out_ref, steps, coefs, values, total
):
    me = lax.axis_index("mode")
    lane = lane_ids(16)
    limit = faces_ref[0]
    for s in range(1, 4):
        limit = jnp.where(me % 4 == FACE_PLACE[s], faces_ref[s], limit)
    live = (lane < 32) & (32 * (me // 4) + lane < limit)
    coefs[...] = jnp.where(live, 0.5 * (klq_ref[...] + remote_ref[128:144, :]), 0.0)
    first = lane_ids(8) < 32
    for s in range(PARTS):
        packed = face_rows(field_ref, s) - remote_ref[8 * s : 8 * s + 8, :]
        for u in range(7):
            piece = jnp.where(first, lanes(packed, -32 * (u % 4)), 0.0)
            row = HERE * s + 4 * u
            steps[row : row + 4, :] = piece[4 * (u // 4) : 4 * (u // 4) + 4]
    total[...] = coefs[0:1, :] * steps[...]
    for k in range(TERMS):
        w = coefs[k + 1 : k + 2, :] * steps[...]
        high = w.astype(BF16).astype(F32)
        values[MODES * k : MODES * k + MODES, :] = (high + lanes(w - high, 32)).astype(BF16)
    for c in range(DEPTH // CHUNK):
        at = pl.ds(c * CHUNK, CHUNK)
        dot = lambda x: jnp.dot(x[:, at], values[at, :], preferred_element_type=F32)
        total[...] += dot(hi_ref) + dot(lo_ref)
    total[...] = total[...] + lanes(total[...], 96)
    group = lane_ids(4) >> 5
    for s in range(PARTS):
        out_ref[s, 0:HERE, :] = main_ref[HERE * s : HERE * s + HERE, :]
        for v in range(2):
            packed = jnp.zeros((4, 128), F32)
            for u in range(4 * v, min(4 * v + 4, 7)):
                flux = total[HERE * s + 4 * u : HERE * s + 4 * u + 4, :]
                packed = jnp.where(group == u % 4, lanes(flux, 32 * (u % 4)), packed)
            out_ref[s, HERE:32, group_of(v)] = packed


def unpack_kernel(count_ref, tiles_ref, cells_ref, far_out, flux, left_hi, left_lo, added, out_ref, left):
    copies = []
    count = count_ref[0]
    sub = lax.broadcasted_iota(jnp.int32, (8, 128), 0)
    group = lane_ids(8) >> 5
    for s in range(4):
        for tau in range(4):
            value = jnp.zeros((8, 128), F32)
            for q in range(4):
                low = tiles_ref[4 * q + FACE_PLACE[s], 24:32, group_of(tau // 2)]
                even = pltpu.roll(lanes(low, 32 * (q - (2 * tau) % 4)), 4, 0)
                odd = lanes(low, 32 * (q - (2 * tau + 1) % 4))
                value = jnp.where(group == q, jnp.where(sub < 4, even, odd), value)
            if tau == 3:
                value = jnp.where(sub < 4, value, 0.0)
            flux[8 * tau : 8 * tau + 8, group_of(s)] = value
    face_row = [cells_ref[s : s + 1, :] >> 7 for s in range(4)]
    high = [flux[:, group_of(s)].astype(BF16).astype(F32) for s in range(4)]
    low = [flux[:, group_of(s)] - high[s] for s in range(4)]
    for r in range(32):
        for s in range(4):
            at = (pl.ds(32 * r, 32), group_of(s))
            left_hi[at] = jnp.where(face_row[s] == r, high[s], 0.0).astype(BF16)
            left_lo[at] = jnp.where(face_row[s] == r, low[s], 0.0).astype(BF16)
    column = lax.broadcasted_iota(jnp.int32, (128, 128), 0)
    pick = jnp.concatenate(
        [jnp.where((cells_ref[s : s + 1, :] & 127) == column, 1.0, 0.0) for s in range(4)], axis=1
    ).astype(BF16)
    spread = lambda x: lax.dot_general(x[...], pick, (((1,), (1,)), ((), ())), preferred_element_type=F32)
    added[...] = spread(left_hi) + spread(left_lo)
    lane = lane_ids(32)
    group = lane >> 5
    for mr in range(4):
        for v in range(2):
            tiles = [tiles_ref[4 * mr + ml, :, group_of(v)] for ml in range(4)]
            for j in range(4):
                row = 8 * mr + 4 * v + j
                value = lanes(tiles[0], -32 * j)
                for ml in range(1, 4):
                    value = jnp.where(group == ml, lanes(tiles[ml], 32 * (ml - j)), value)
                value = value + added[32 * row : 32 * row + 32, :]
                value = jnp.where(lane + 128 * row < count, value, 0.0)
                out_ref[:, group_of(row)] = value[0:HERE]
        at = pl.ds(1024 * mr, 1024)
        copies.append(pltpu.make_async_copy(out_ref.at[:, at], far_out.at[:, at], left.at[mr]))
        copies[mr].start()
    for copy in copies:
        copy.wait()


def face_route(blocks):
    route = []
    for b in range(blocks):
        for s, offset in enumerate(SLOT_OFFSETS):
            if 0 <= b + offset < blocks:
                for q in range(4):
                    source, target = 4 * q + FACE_PLACE[s], 4 * q + FACE_PLACE[3 - s]
                    route.append((16 * b + source, 16 * (b + offset) + target))
    return route


VMEM = pl.BlockSpec(memory_space=pltpu.VMEM)
SMEM = pl.BlockSpec(memory_space=pltpu.SMEM)
HBM = pl.BlockSpec(memory_space=pl.ANY)


def kernel_call(body, name, shapes, in_specs, scratch, micros, limit, place=None):
    return pl.pallas_call(
        body,
        out_shape=shapes,
        in_specs=in_specs,
        out_specs=tuple(VMEM for _ in shapes) if isinstance(shapes, tuple) else place or VMEM,
        scratch_shapes=scratch,
        compiler_params=pltpu.CompilerParams(vmem_limit_bytes=limit << 20),
        cost_estimate=pl.CostEstimate(flops=int(micros * 1e9), bytes_accessed=int(micros * 1e6), transcendentals=0),
        name=name,
    )


def array(*shape):
    return jax.ShapeDtypeStruct(shape, F32)


def per_device(chaos_field, kl_field, partner, chaos_coef, cell_count, face_count, face_cells):
    cells = face_cells[0]
    far = lambda each: pltpu.with_memory_space_constraint(each, pltpu.HBM)
    send, coefs, klq = kernel_call(
        pack_kernel,
        "pack",
        (array(PARTS, 32, 384), array(4, 16, 256), array(16, 128)),
        [SMEM, HBM, HBM, HBM, HBM, HBM],
        [
            pltpu.VMEM(cells.shape, jnp.int32),
            pltpu.VMEM((HERE, 4096), F32),
            pltpu.VMEM(kl_field.shape, F32),
            pltpu.VMEM((16, 4096), F32),
            pltpu.VMEM(partner.shape, jnp.int32),
            pltpu.VMEM(chaos_coef.shape, F32),
            pltpu.VMEM((128, 128), F32),
            pltpu.SemaphoreType.DMA((8,)),
        ],
        4,
        8,
    )(cell_count, far(chaos_field), far(kl_field), far(cells), far(partner), far(chaos_coef))
    field = lax.all_to_all(send, "mode", 0, 0, tiled=True)
    outgoing = kernel_call(outgoing_kernel, "outgoing", array(144, 128), [VMEM] * 2, [], 0.5, 4)(field, klq)
    remote = lax.ppermute(outgoing, ("blk", "mode"), face_route(lax.axis_size("blk")))
    mix = jax.ShapeDtypeStruct((MODES, DEPTH), BF16)
    main, mix_hi, mix_lo = kernel_call(
        apply_kernel,
        "apply",
        (array(MODES, 256), mix, mix),
        [VMEM] * 2,
        [
            pltpu.VMEM((4, MODES, 256), F32),
            pltpu.VMEM((MODES, 384), F32),
            pltpu.VMEM((DEPTH, 256), BF16),
            pltpu.VMEM((DEPTH, 256), BF16),
        ],
        8,
        24,
    )(field, coefs)
    tiles = kernel_call(
        flux_kernel,
        "flux",
        array(PARTS, 32, 256),
        [SMEM] + [VMEM] * 6,
        [
            pltpu.VMEM((MODES, 128), F32),
            pltpu.VMEM((16, 128), F32),
            pltpu.VMEM((DEPTH, 128), BF16),
            pltpu.VMEM((MODES, 128), F32),
        ],
        4,
        8,
    )(face_count[0], field, remote, klq, main, mix_hi, mix_lo)
    back = lax.all_to_all(tiles, "mode", 0, 0, tiled=True)
    return kernel_call(
        unpack_kernel,
        "unpack",
        jax.ShapeDtypeStruct(chaos_field.shape, F32),
        [SMEM, VMEM, VMEM],
        [
            pltpu.VMEM((32, 512), F32),
            pltpu.VMEM((1024, 512), BF16),
            pltpu.VMEM((1024, 512), BF16),
            pltpu.VMEM((1024, 128), F32),
            pltpu.VMEM((HERE, 4096), F32),
            pltpu.SemaphoreType.DMA((4,)),
        ],
        3,
        8,
        HBM,
    )(cell_count, back, cells)


def solution(mesh):
    in_specs = (
        P("mode", "blk"),
        P(None, "blk"),
        P(None, None, "mode"),
        P(None, None, "mode"),
        P("blk"),
        P("blk", None),
        P("blk", None, None),
    )
    return jax.shard_map(
        per_device, mesh=mesh, in_specs=in_specs, out_specs=P("mode", "blk"), check_vma=False
    )
```
